512 devices in a mesh: sensor: 128 (over y, z, core), step: 4 (over x).
Axes of the slice: x: 4, y: 4, z: 16, core: 2. Of those that a mesh axis runs over, the one named last changes fastest.
Arguments:
- inputs: bfloat16 [12, 8192, 512], P('step', 'sensor'), may hold values from -6 to 6
- cotangent: bfloat16 [12, 8192, 512], P('step', 'sensor'), may hold values from -6 to 6
- w_query: bfloat16 [512, 512], replicated, may hold values from -0.25 to 0.25
- w_key: bfloat16 [512, 512], replicated, may hold values from -0.25 to 0.25
- w_value: bfloat16 [512, 512], replicated, may hold values from -0.25 to 0.25
- w_up: bfloat16 [512, 256], replicated, may hold values from -0.25 to 0.25
- w_down: bfloat16 [256, 512], replicated, may hold values from -0.375 to 0.375
- feature_proj: float32 [8, 64, 64], replicated, may hold values from -5 to 5
- live_count: int32 [128], P('sensor'), may hold values from 32 to 64, as said below
Outputs:
- grad_inputs: bfloat16 [12, 8192, 512], P('step', 'sensor')
- grad_query: float32 [512, 512], P('sensor', 'step')
- grad_key: float32 [512, 512], P('sensor', 'step')
- grad_value: float32 [512, 512], P('sensor', 'step')
The draws below stay inside these ranges and needn't reach their ends.
Inputs may be any that keep to these rules, and one draw needn't show every extreme that they name: `live_count`: some group has all 64 sensors live; every group has at least half of them live.
All inputs are finite; a program needn't handle non-finite values.
Results may differ from the reference program's by a relative error of at most 0.012.
Values sent between devices are 32-bit elements; how exact they have to be, the bound alone decides.
A program may use at most 64 MiB of HBM per device.

```python
import math
import jax
import jax.numpy as jnp
from jax import lax

H = 8
E = 64
D = 512
R = 64
F = 256
SENS_DEV = 64
STEPS = 12
SENSORS = 8192
N_SENSOR = 128


def draw_live_count(key, part):
    counts = jax.random.randint(jax.random.fold_in(key, 11), (N_SENSOR,), SENS_DEV // 2, SENS_DEV + 1)
    chosen = jax.random.randint(jax.random.fold_in(key, 12), (), 0, N_SENSOR)
    return jnp.where(jnp.arange(N_SENSOR) == chosen, SENS_DEV, counts).astype(jnp.int32)


def block_scale(key, dims, pieces, least, largest):
    def one(dim, blocks):
        draws = jax.random.uniform(jax.random.fold_in(jax.random.fold_in(key, 6), dim), (blocks,), jnp.float32, least / len(pieces), largest / len(pieces))
        return jnp.repeat(jnp.exp(draws), dims[dim] // blocks).reshape((-1,) + (1,) * (len(dims) - dim - 1))

    factor_of = one(*pieces[0])
    for cut in pieces[1:]:
        factor_of = factor_of * one(*cut)
    return factor_of


def noise(rng, shape, deviation, most, shards=(), kind=jnp.bfloat16):
    values = jax.random.normal(rng, shape, jnp.float32) * deviation
    if len(shards) > 0:
        values = block_scale(rng, shape, shards, -0.22, 0.18) * values
    return jnp.clip(values, min=-most, max=most).astype(kind)


def setup_inputs(seed: int = 0) -> dict:
    streams_of = jax.random.split(jax.random.key(seed), 10)
    inputs = noise(streams_of[0], (STEPS, SENSORS, D), 1.0, 6.0, ((0, 4), (1, 128)))
    cotangent = noise(streams_of[1], (STEPS, SENSORS, D), 1.0, 6.0, ((0, 4), (1, 128)))
    w_query = noise(streams_of[2], (D, D), D ** -0.5, 0.25)
    w_key = noise(streams_of[3], (D, D), D ** -0.5, 0.25)
    w_value = noise(streams_of[4], (D, D), D ** -0.5, 0.25)
    w_up = noise(streams_of[5], (D, F), D ** -0.5, 0.25)
    w_down = noise(streams_of[6], (F, D), F ** -0.5, 0.375)
    feature_proj = noise(streams_of[7], (H, E, R), 1.0, 5.0, (), jnp.float32)
    live_count = draw_live_count(jax.random.fold_in(streams_of[9], 71), 0)
    return dict(inputs=inputs, cotangent=cotangent, w_query=w_query, w_key=w_key, w_value=w_value, w_up=w_up, w_down=w_down, feature_proj=feature_proj, live_count=live_count)


HIGH = lax.Precision.HIGHEST

def feature_map(scaled, feature_proj):
    projected = jnp.einsum('...he,her->...hr', scaled, feature_proj, precision=HIGH)
    return jnp.exp(projected - 0.5 * lax.optimization_barrier(jnp.sum(scaled * scaled, -1, keepdims=True))) * feature_proj.shape[2] ** (-0.5)

def feature_back(incoming, feat, scaled, feature_proj):
    weighted = incoming * feat
    return jnp.einsum('...hr,her->...he', weighted, feature_proj, precision=HIGH) - scaled * lax.optimization_barrier(jnp.sum(weighted, -1, keepdims=True))

def step_grads(inputs, cotangent, valid, w_query, w_key, w_value, w_up, w_down, feature_proj):
    sensors, width = inputs.shape
    heads, head_dim, feats = feature_proj.shape
    factor = head_dim ** (-0.25)

    def project(weight):
        return jnp.dot(inputs, weight, preferred_element_type=jnp.float32).reshape(sensors, heads, head_dim)
    scaled_query = project(w_query) * factor
    scaled_key = project(w_key) * factor
    values = project(w_value)
    feat_query = feature_map(scaled_query, feature_proj)
    feat_key = feature_map(scaled_key, feature_proj)
    masked_key = feat_key * valid[:, None, None]
    summary = jnp.einsum('nhr,nhe->hre', masked_key, values, precision=HIGH)
    normal_sum = lax.optimization_barrier(jnp.sum(masked_key, 0))
    numer = jnp.einsum('nhr,hre->nhe', feat_query, summary, precision=HIGH)
    denom = jnp.einsum('nhr,hr->nh', feat_query, normal_sum, precision=HIGH)
    attended = numer / denom[..., None]
    flat_att = attended.reshape(sensors, width)
    rms_val = jnp.sqrt(lax.optimization_barrier(jnp.mean(flat_att * flat_att, -1, keepdims=True)) + 1e-06)
    normed = flat_att / rms_val
    pre_act = jnp.dot(normed.astype(jnp.bfloat16), w_up, preferred_element_type=jnp.float32)
    masked_cot = cotangent * valid.astype(jnp.bfloat16)[:, None]
    grad_hidden = jnp.dot(masked_cot, w_down.T, preferred_element_type=jnp.float32)
    _, gelu_back = jax.vjp(jax.nn.gelu, pre_act)
    grad_pre = gelu_back(grad_hidden)[0].astype(jnp.bfloat16)
    grad_normed = jnp.dot(grad_pre, w_up.T, preferred_element_type=jnp.float32)
    grad_att = (grad_normed - normed * lax.optimization_barrier(jnp.mean(grad_normed * normed, -1, keepdims=True))) / rms_val
    grad_att = grad_att.reshape(sensors, heads, head_dim)
    grad_num = grad_att / denom[..., None]
    grad_den = -lax.optimization_barrier(jnp.sum(grad_att * attended, -1)) / denom
    grad_fq = jnp.einsum('nhe,hre->nhr', grad_num, summary, precision=HIGH) + grad_den[..., None] * normal_sum[None]
    grad_summary = jnp.einsum('nhr,nhe->hre', feat_query, grad_num, precision=HIGH)
    grad_normal = jnp.einsum('nhr,nh->hr', feat_query, grad_den, precision=HIGH)
    grad_fk = (jnp.einsum('nhe,hre->nhr', values, grad_summary, precision=HIGH) + grad_normal[None]) * valid[:, None, None]
    grad_val = jnp.einsum('nhr,hre->nhe', masked_key, grad_summary, precision=HIGH)
    grad_q = feature_back(grad_fq, feat_query, scaled_query, feature_proj) * factor
    grad_k = feature_back(grad_fk, feat_key, scaled_key, feature_proj) * factor
    grad_q = grad_q.reshape(sensors, width).astype(jnp.bfloat16)
    grad_k = grad_k.reshape(sensors, width).astype(jnp.bfloat16)
    grad_val = grad_val.reshape(sensors, width).astype(jnp.bfloat16)
    grad_in = jnp.dot(grad_q, w_query.T, preferred_element_type=jnp.float32)
    grad_in = grad_in + jnp.dot(grad_k, w_key.T, preferred_element_type=jnp.float32)
    grad_in = grad_in + jnp.dot(grad_val, w_value.T, preferred_element_type=jnp.float32)
    weight_q = jnp.dot(inputs.T, grad_q, preferred_element_type=jnp.float32)
    weight_k = jnp.dot(inputs.T, grad_k, preferred_element_type=jnp.float32)
    weight_v = jnp.dot(inputs.T, grad_val, preferred_element_type=jnp.float32)
    return (grad_in.astype(jnp.bfloat16), (weight_q, weight_k, weight_v))

def reference(inputs, cotangent, w_query, w_key, w_value, w_up, w_down, feature_proj, live_count):
    sensors = inputs.shape[1]
    width = inputs.shape[2]
    position = jnp.arange(sensors, dtype=jnp.int32)
    valid = (position % SENS_DEV < live_count[position // SENS_DEV]).astype(jnp.float32)
    zeros = jnp.zeros((width, width), jnp.float32)

    def advance(carry, pair):
        grad_in, grads = step_grads(pair[0], pair[1], valid, w_query, w_key, w_value, w_up, w_down, feature_proj)
        return ((carry[0] + grads[0], carry[1] + grads[1], carry[2] + grads[2]), grad_in)
    totals, grad_inputs = lax.scan(advance, (zeros, zeros, zeros), (inputs, cotangent))
    norm_scale = 1.0 / math.sqrt(inputs.shape[0] * sensors)
    return (grad_inputs, totals[0] * norm_scale, totals[1] * norm_scale, totals[2] * norm_scale)
```

```python
import functools
import math

import jax
import jax.numpy as jnp
from jax import lax
from jax.experimental import pallas as pl
from jax.experimental.pallas import tpu as pltpu
from jax.sharding import PartitionSpec as P

MESH = pl.DeviceIdType.MESH
VM = pl.BlockSpec(memory_space=pltpu.VMEM)


def place(grid):
    _, zs, _ = grid
    s = lax.axis_index("sensor")
    return lax.axis_index("step"), s // (2 * zs), lax.rem(s // 2, zs), lax.rem(s, 2)


def at(grid, x, y, z, c):
    return ((y * grid[1] + z) * 2 + c, x)


def send(src, dst, ssem, rsem, target):
    copy = pltpu.make_async_remote_copy(
        src_ref=src, dst_ref=dst, send_sem=ssem, recv_sem=rsem, device_id=target, device_id_type=MESH
    )
    return copy


def greet(targets):
    barrier = pltpu.get_barrier_semaphore()
    for target in targets:
        pl.semaphore_signal(barrier, inc=1, device_id=target, device_id_type=MESH)
    pl.semaphore_wait(barrier, len(targets))


def all_reduce_kernel(grid, x_ref, out_ref, buf_c, acc_c, buf_y, acc_y, buf_z, sc, rc, sy, ry, sz, rz):
    ys, zs, _ = grid
    tiles = x_ref.shape[2]
    x, y, z, c = place(grid)
    partner = at(grid, x, y, z, 1 - c)
    y_peer = [at(grid, x, lax.rem(y + d, ys), z, c) for d in range(1, ys)]
    z_peer = [at(grid, x, y, lax.rem(z + d, zs), c) for d in range(1, zs)]
    greet([partner] + y_peer + z_peer)

    pair = send(x_ref.at[1 - c], buf_c, sc.at[0], rc.at[0], partner)
    pair.start()
    pair.wait()
    acc_c[...] = x_ref[c] + buf_c[...]

    down = [
        send(acc_c.at[lax.rem(y + d, ys)], buf_y.at[d - 1], sy.at[0, d - 1], ry.at[0, d - 1], y_peer[d - 1])
        for d in range(1, ys)
    ]
    for copy in down:
        copy.start()
    for copy in down:
        copy.wait()
    acc_y[...] = acc_c[y] + sum(buf_y[d - 1] for d in range(1, ys))

    for d in range(1, zs):
        other = lax.rem(z + d, zs)

        @pl.when(other < tiles)
        def _():
            send(acc_y.at[other], buf_z.at[d - 1], sz.at[0, d - 1], rz.at[0, d - 1], z_peer[d - 1]).start()

    @pl.when(z < tiles)
    def _():
        for d in range(1, zs):
            send(acc_y.at[0], buf_z.at[d - 1], sz.at[0, d - 1], rz.at[0, d - 1], z_peer[d - 1]).wait_recv()
        out_ref[c, y, z] = acc_y[z] + sum(buf_z[d - 1] for d in range(1, zs))
        for d in range(1, zs):
            mine = out_ref.at[c, y, z]
            send(mine, mine, sz.at[1, d - 1], rz.at[1, d - 1], z_peer[d - 1]).start()

    for d in range(1, zs):
        other = lax.rem(z + d, zs)

        @pl.when(other < tiles)
        def _():
            send(acc_y.at[other], buf_z.at[d - 1], sz.at[0, d - 1], rz.at[0, d - 1], z_peer[d - 1]).wait_send()

    for d in range(1, zs):
        source = lax.rem(z + zs - d, zs)

        @pl.when(source < tiles)
        def _():
            theirs = out_ref.at[c, y, source]
            send(theirs, theirs, sz.at[1, d - 1], rz.at[1, d - 1], z_peer[d - 1]).wait_recv()

    up = []
    for d in range(1, ys):
        mine = out_ref.at[c, y]
        up.append(send(mine, mine, sy.at[1, d - 1], ry.at[1, d - 1], y_peer[d - 1]))
    for copy in up:
        copy.start()
    for copy in up:
        copy.wait()
    mine = out_ref.at[c]
    pair = send(mine, mine, sc.at[1], rc.at[1], partner)
    pair.start()

    @pl.when(z < tiles)
    def _():
        for d in range(1, zs):
            mine = out_ref.at[c, y, z]
            send(mine, mine, sz.at[1, d - 1], rz.at[1, d - 1], z_peer[d - 1]).wait_send()

    pair.wait()


def all_reduce(data, grid, ident):
    ys, zs, _ = grid
    _, _, tiles, rows, lanes = data.shape
    dma = pltpu.SemaphoreType.DMA
    block = (rows, lanes)
    return pl.pallas_call(
        functools.partial(all_reduce_kernel, grid),
        out_shape=jax.ShapeDtypeStruct(data.shape, jnp.float32),
        in_specs=[VM],
        out_specs=VM,
        scratch_shapes=[
            pltpu.VMEM((ys, tiles) + block, jnp.float32),
            pltpu.VMEM((ys, tiles) + block, jnp.float32),
            pltpu.VMEM((ys - 1, tiles) + block, jnp.float32),
            pltpu.VMEM((tiles,) + block, jnp.float32),
            pltpu.VMEM((zs - 1,) + block, jnp.float32),
            dma((2,)),
            dma((2,)),
            dma((2, ys - 1)),
            dma((2, ys - 1)),
            dma((2, zs - 1)),
            dma((2, zs - 1)),
        ],
        compiler_params=pltpu.CompilerParams(collective_id=ident, has_side_effects=True, vmem_limit_bytes=32 << 20),
    )(data)


def scatter_kernel(
    grid, scale, xf_ref, yf_ref, out_ref, xp, yp, xq, yq, xr, yr, xb, yb, xs, ys_, zsrc, zbuf,
    s1, r1, s2, r2, s3, r3, sz, rz,
):
    ys, zs, xs_n = grid
    x, y, z, c = place(grid)
    partner = at(grid, x, y, z, 1 - c)
    x_peer = [at(grid, lax.rem(x + d, xs_n), y, z, c) for d in range(1, xs_n)]
    y_peer = [at(grid, x, lax.rem(y + d, ys), z, c) for d in range(1, ys)]
    z_peer = [at(grid, x, y, lax.rem(z + d, zs), c) for d in range(1, zs)]
    greet([partner] + x_peer + y_peer + z_peer)

    first = [
        send(xf_ref.at[1 - c], xp, s1.at[0], r1.at[0], partner),
        send(yf_ref.at[1 - c], yp, s1.at[1], r1.at[1], partner),
    ]
    for copy in first:
        copy.start()
    first[0].wait()
    xq[...] = xf_ref[c] + xp[...]
    second_x = [
        send(xq.at[lax.rem(x + d, xs_n)], xr.at[d - 1], s2.at[0, d - 1], r2.at[0, d - 1], x_peer[d - 1])
        for d in range(1, xs_n)
    ]
    for copy in second_x:
        copy.start()
    first[1].wait()
    yq[...] = yf_ref[c] + yp[...]
    second_y = [
        send(yq.at[lax.rem(y + d, ys)], yr.at[d - 1], s2.at[1, d - 1], r2.at[1, d - 1], y_peer[d - 1])
        for d in range(1, ys)
    ]
    for copy in second_y:
        copy.start()
    for copy in second_x:
        copy.wait()
    xs[...] = xq[x] + sum(xr[d - 1] for d in range(1, xs_n))
    third_y = [
        send(xs.at[lax.rem(y + d, ys)], xb.at[d - 1], s3.at[0, d - 1], r3.at[0, d - 1], y_peer[d - 1])
        for d in range(1, ys)
    ]
    for copy in third_y:
        copy.start()
    for copy in second_y:
        copy.wait()
    ys_[...] = yq[y] + sum(yr[d - 1] for d in range(1, ys))
    third_x = [
        send(ys_.at[lax.rem(x + d, xs_n)], yb.at[d - 1], s3.at[1, d - 1], r3.at[1, d - 1], x_peer[d - 1])
        for d in range(1, xs_n)
    ]
    for copy in third_x:
        copy.start()
    for copy in third_y:
        copy.wait()
    half = zs // 2
    weights = xs.shape[1]
    low = xs[y] + sum(xb[d - 1] for d in range(1, ys))
    for w in range(weights):
        zsrc[0:half, w] = low[w].reshape(half, 4, 128)
    for copy in third_x:
        copy.wait()
    high = ys_[x] + sum(yb[d - 1] for d in range(1, xs_n))
    for w in range(weights):
        zsrc[half:zs, w] = high[w].reshape(half, 4, 128)
    last = [
        send(zsrc.at[lax.rem(z + d, zs)], zbuf.at[d - 1], sz.at[d - 1], rz.at[d - 1], z_peer[d - 1])
        for d in range(1, zs)
    ]
    for copy in last:
        copy.start()
    for copy in last:
        copy.wait()
    out_ref[...] = (zsrc[z] + sum(zbuf[d - 1] for d in range(1, zs))) * scale


def scatter_sum(x_first, y_first, grid, scale, ident):
    ys, zs, xs = grid
    weights, rows, lanes = x_first.shape[3:]
    dma = pltpu.SemaphoreType.DMA
    block = (weights, rows, lanes)
    f32 = jnp.float32
    return pl.pallas_call(
        functools.partial(scatter_kernel, grid, scale),
        out_shape=jax.ShapeDtypeStruct((weights, 4, lanes), f32),
        in_specs=[VM, VM],
        out_specs=VM,
        scratch_shapes=[
            pltpu.VMEM((xs, ys) + block, f32),
            pltpu.VMEM((ys, xs) + block, f32),
            pltpu.VMEM((xs, ys) + block, f32),
            pltpu.VMEM((ys, xs) + block, f32),
            pltpu.VMEM((xs - 1, ys) + block, f32),
            pltpu.VMEM((ys - 1, xs) + block, f32),
            pltpu.VMEM((ys - 1,) + block, f32),
            pltpu.VMEM((xs - 1,) + block, f32),
            pltpu.VMEM((ys,) + block, f32),
            pltpu.VMEM((xs,) + block, f32),
            pltpu.VMEM((zs, weights, 4, lanes), f32),
            pltpu.VMEM((zs - 1, weights, 4, lanes), f32),
            dma((2,)),
            dma((2,)),
            dma((2, max(xs, ys) - 1)),
            dma((2, max(xs, ys) - 1)),
            dma((2, max(xs, ys) - 1)),
            dma((2, max(xs, ys) - 1)),
            dma((zs - 1,)),
            dma((zs - 1,)),
        ],
        compiler_params=pltpu.CompilerParams(collective_id=ident, has_side_effects=True, vmem_limit_bytes=48 << 20),
    )(x_first, y_first)

HIGH = lax.Precision.HIGHEST
YS, ZS, XS = 4, 16, 4
GRID = (YS, ZS, XS)


def sum_over_sensors(summary, normal, ident):
    steps, heads, feats, width = summary.shape
    tiles = summary.reshape(steps, heads // 2, 2, feats, width).transpose(0, 1, 3, 2, 4)
    tiles = tiles.reshape(2, YS, 12, 8, 128)
    extra = jnp.pad(normal.reshape(12, 128), ((0, 4), (0, 0))).reshape(2, YS, 1, 2, 128)
    extra = jnp.pad(extra, ((0, 0), (0, 0), (0, 0), (0, 6), (0, 0)))
    total = all_reduce(jnp.concatenate((tiles, extra), 2), GRID, ident)
    summed = total[:, :, :12].reshape(steps, heads // 2, feats, 2, width).transpose(0, 1, 3, 2, 4)
    normal_sum = total[:, :, 12, :2].reshape(16, 128)[:12]
    return summed.reshape(summary.shape), normal_sum.reshape(normal.shape)


def feature_map(scaled, feature_proj):
    projected = jnp.einsum("...he,her->...hr", scaled, feature_proj, precision=HIGH)
    return jnp.exp(
        projected - 0.5 * jnp.sum(scaled * scaled, -1, keepdims=True)
    ) * feature_proj.shape[2] ** (-0.5)


def feature_back(incoming, feat, scaled, feature_proj):
    weighted = incoming * feat
    return jnp.einsum(
        "...hr,her->...he", weighted, feature_proj, precision=HIGH
    ) - scaled * jnp.sum(weighted, -1, keepdims=True)


def shards(inputs, cotangent, w_query, w_key, w_value, w_up, w_down, feature_proj, live_count):
    steps_here, sensors_here, width = inputs.shape
    heads, head_dim, feats = feature_proj.shape
    factor = head_dim ** (-0.25)
    valid = (jnp.arange(sensors_here, dtype=jnp.int32) < live_count[0]).astype(jnp.float32)
    flat_in = inputs.reshape(steps_here * sensors_here, width)

    def project(weight):
        return jnp.dot(flat_in, weight, preferred_element_type=jnp.float32).reshape(
            steps_here, sensors_here, heads, head_dim
        )

    scaled_query = project(w_query) * factor
    scaled_key = project(w_key) * factor
    values = project(w_value)
    feat_query = feature_map(scaled_query, feature_proj)
    feat_key = feature_map(scaled_key, feature_proj)
    masked_key = feat_key * valid[None, :, None, None]
    local_summary = jnp.einsum("tnhr,tnhe->thre", masked_key, values, precision=HIGH)
    local_normal = jnp.sum(masked_key, 1)
    summary, normal_sum = sum_over_sensors(local_summary, local_normal, 0)
    numer = jnp.einsum("tnhr,thre->tnhe", feat_query, summary, precision=HIGH)
    denom = jnp.einsum("tnhr,thr->tnh", feat_query, normal_sum, precision=HIGH)
    attended = numer / denom[..., None]
    flat_att = attended.reshape(steps_here * sensors_here, width)
    rms_val = jnp.sqrt(jnp.mean(flat_att * flat_att, -1, keepdims=True) + 1e-06)
    normed = flat_att / rms_val
    pre_act = jnp.dot(normed.astype(jnp.bfloat16), w_up, preferred_element_type=jnp.float32)
    masked_cot = (cotangent * valid.astype(jnp.bfloat16)[None, :, None]).reshape(
        steps_here * sensors_here, width
    )
    grad_hidden = jnp.dot(masked_cot, w_down.T, preferred_element_type=jnp.float32)
    _, gelu_back = jax.vjp(jax.nn.gelu, pre_act)
    grad_pre = gelu_back(grad_hidden)[0].astype(jnp.bfloat16)
    grad_normed = jnp.dot(grad_pre, w_up.T, preferred_element_type=jnp.float32)
    grad_att = (grad_normed - normed * jnp.mean(grad_normed * normed, -1, keepdims=True)) / rms_val
    grad_att = grad_att.reshape(steps_here, sensors_here, heads, head_dim)
    grad_num = grad_att / denom[..., None]
    grad_den = -jnp.sum(grad_att * attended, -1) / denom
    grad_fq = (
        jnp.einsum("tnhe,thre->tnhr", grad_num, summary, precision=HIGH)
        + grad_den[..., None] * normal_sum[:, None]
    )
    local_gsum = jnp.einsum("tnhr,tnhe->thre", feat_query, grad_num, precision=HIGH)
    local_gnorm = jnp.einsum("tnhr,tnh->thr", feat_query, grad_den, precision=HIGH)
    grad_summary, grad_normal = sum_over_sensors(local_gsum, local_gnorm, 1)
    grad_fk = (
        jnp.einsum("tnhe,thre->tnhr", values, grad_summary, precision=HIGH) + grad_normal[:, None]
    ) * valid[None, :, None, None]
    grad_val = jnp.einsum("tnhr,thre->tnhe", masked_key, grad_summary, precision=HIGH)
    grad_q = feature_back(grad_fq, feat_query, scaled_query, feature_proj) * factor
    grad_k = feature_back(grad_fk, feat_key, scaled_key, feature_proj) * factor
    flat_rows = steps_here * sensors_here
    grad_q = grad_q.reshape(flat_rows, width).astype(jnp.bfloat16)
    grad_k = grad_k.reshape(flat_rows, width).astype(jnp.bfloat16)
    grad_val = grad_val.reshape(flat_rows, width).astype(jnp.bfloat16)
    grad_in = jnp.dot(grad_q, w_query.T, preferred_element_type=jnp.float32)
    grad_in = grad_in + jnp.dot(grad_k, w_key.T, preferred_element_type=jnp.float32)
    grad_in = grad_in + jnp.dot(grad_val, w_value.T, preferred_element_type=jnp.float32)
    grad_inputs = grad_in.astype(jnp.bfloat16).reshape(steps_here, sensors_here, width)
    weight_q = jnp.einsum("nd,nk->dk", flat_in, grad_q, preferred_element_type=jnp.float32)
    weight_k = jnp.einsum("nd,nk->dk", flat_in, grad_k, preferred_element_type=jnp.float32)
    weight_v = jnp.einsum("nd,nk->dk", flat_in, grad_val, preferred_element_type=jnp.float32)
    total_rows = steps_here * lax.axis_size("step") * sensors_here * lax.axis_size("sensor")
    norm_scale = 1.0 / math.sqrt(total_rows)
    stacked = jnp.stack((weight_q, weight_k, weight_v)).reshape(3, YS, 2, ZS // 2, 2, 4, XS, 128)
    x_first = stacked[:, :, 0].transpose(3, 5, 1, 0, 2, 4, 6).reshape(2, XS, YS, 3, ZS * 2, 128)
    y_first = stacked[:, :, 1].transpose(3, 1, 5, 0, 2, 4, 6).reshape(2, YS, XS, 3, ZS * 2, 128)
    reduced = scatter_sum(x_first, y_first, GRID, norm_scale, 2)
    return (grad_inputs, reduced[0], reduced[1], reduced[2])


def solution(mesh):
    placed = (
        P("step", "sensor", None),
        P("step", "sensor", None),
        P(),
        P(),
        P(),
        P(),
        P(),
        P(),
        P("sensor"),
    )
    return jax.shard_map(
        shards,
        mesh=mesh,
        in_specs=placed,
        out_specs=(
            P("step", "sensor", None),
            P("sensor", "step"),
            P("sensor", "step"),
            P("sensor", "step"),
        ),
        check_vma=False,
    )
```

```python
import functools
import math

import jax
import jax.numpy as jnp
from jax import lax
from jax.experimental import pallas as pl
from jax.experimental.pallas import tpu as pltpu
from jax.sharding import PartitionSpec as P

MESH = pl.DeviceIdType.MESH
VM = pl.BlockSpec(memory_space=pltpu.VMEM)
SM = pl.BlockSpec(memory_space=pltpu.SMEM)
F32, BF16 = jnp.float32, jnp.bfloat16
YS, ZS, XS = 4, 16, 4
T, N, D, F, H, E = 3, 64, 512, 256, 8, 64
ROWS = T * N
PAIRS = H // 2
TILES = 13
QUAD = 256
FACTOR = E ** (-0.25)


def at(x, y, z, c):
    return ((y * ZS + z) * 2 + c, x)


def send(src, dst, ssem, rsem, target):
    return pltpu.make_async_remote_copy(
        src_ref=src, dst_ref=dst, send_sem=ssem, recv_sem=rsem, device_id=target, device_id_type=MESH
    )


def start(copies):
    for copy in copies:
        copy.start()


def wait(copies):
    for copy in copies:
        copy.wait()


def dot(a, b):
    return lax.dot_general(a, b, (((1,), (0,)), ((), ())), preferred_element_type=F32)


def dot_nt(a, b):
    return lax.dot_general(a, b, (((1,), (1,)), ((), ())), preferred_element_type=F32)


def dot_tn(a, b):
    return lax.dot_general(a, b, (((0,), (0,)), ((), ())), preferred_element_type=F32)


def split(value):
    high = value.astype(BF16)
    return high, (value - high.astype(F32)).astype(BF16)


def dot3(product, a, b):
    return product(a[0], b[0]) + product(a[1], b[0]) + product(a[0], b[1])


def head_sum(value, ones):
    high, low = split(value)
    return dot(high, ones) + dot(low, ones)


def gelu_slope(v):
    k = math.sqrt(2 / math.pi)
    th = jnp.tanh(k * (v + 0.044715 * v * v * v))
    return 0.5 * (1.0 + th) + 0.5 * v * (1.0 - th * th) * (k * (1.0 + 3 * 0.044715 * v * v))


class Reduce:
    def __init__(self, pos, peers, r, tag):
        self.pos, self.peers = pos, peers
        self.x, self.out = r["x" + tag], r["out" + tag]
        self.buf_c, self.acc_c = r["bufc" + tag], r["accc" + tag]
        self.buf_y, self.acc_y, self.buf_z = r["bufy" + tag], r["accy" + tag], r["bufz" + tag]
        self.sc, self.rc, self.sy, self.ry = r["sc" + tag], r["rc" + tag], r["sy" + tag], r["ry" + tag]
        self.sz, self.rz = r["sz" + tag], r["rz" + tag]

    def start_core(self):
        c = self.pos[3]
        self.core = send(self.x.at[1 - c], self.buf_c, self.sc.at[0], self.rc.at[0], self.peers["c"])
        self.core.start()

    def start_y(self):
        _, y, _, c = self.pos
        self.core.wait()
        self.acc_c[...] = self.x[c] + self.buf_c[...]
        self.down = [
            send(
                self.acc_c.at[lax.rem(y + d, YS)], self.buf_y.at[d - 1], self.sy.at[0, d - 1], self.ry.at[0, d - 1],
                self.peers["y"][d - 1],
            )
            for d in range(1, YS)
        ]
        start(self.down)

    def z_down(self, d, slot):
        return send(
            self.acc_y.at[slot], self.buf_z.at[d - 1], self.sz.at[0, d - 1], self.rz.at[0, d - 1], self.peers["z"][d - 1]
        )

    def z_up(self, d, slot):
        piece = self.out.at[self.pos[3], self.pos[1], slot]
        return send(piece, piece, self.sz.at[1, d - 1], self.rz.at[1, d - 1], self.peers["z"][d - 1])

    def start_z(self):
        _, y, z, _ = self.pos
        wait(self.down)
        self.acc_y[...] = self.acc_c[y] + self.buf_y[0] + self.buf_y[1] + self.buf_y[2]
        for d in range(1, ZS):
            other = lax.rem(z + d, ZS)

            @pl.when(other < TILES)
            def _():
                self.z_down(d, other).start()

    def start_z_back(self):
        _, y, z, c = self.pos

        @pl.when(z < TILES)
        def _():
            for d in range(1, ZS):
                self.z_down(d, 0).wait_recv()
            self.out[c, y, z] = self.acc_y[z] + sum(self.buf_z[d - 1] for d in range(1, ZS))
            for d in range(1, ZS):
                self.z_up(d, z).start()

    def start_y_back(self):
        _, y, z, c = self.pos
        for d in range(1, ZS):
            source = lax.rem(z + ZS - d, ZS)

            @pl.when(source < TILES)
            def _():
                self.z_up(d, source).wait_recv()

        mine = self.out.at[c, y]
        self.up = [
            send(mine, mine, self.sy.at[1, d - 1], self.ry.at[1, d - 1], self.peers["y"][d - 1]) for d in range(1, YS)
        ]
        start(self.up)

    def start_core_back(self):
        c = self.pos[3]
        wait(self.up)
        mine = self.out.at[c]
        self.core = send(mine, mine, self.sc.at[1], self.rc.at[1], self.peers["c"])
        self.core.start()

    def finish(self):
        self.core.wait()

    def drain(self):
        z = self.pos[2]
        for d in range(1, ZS):
            other = lax.rem(z + d, ZS)

            @pl.when(other < TILES)
            def _():
                self.z_down(d, other).wait_send()

        @pl.when(z < TILES)
        def _():
            for d in range(1, ZS):
                self.z_up(d, z).wait_send()


def tile_place(tile):
    group, slot = divmod(tile, 12)
    return group // YS, group % YS, slot


def put_blocks(ref, moment, quad, result):
    first = lax.broadcasted_iota(jnp.int32, (E, 128), 1) < E
    for j in range(2):
        part = result[128 * j : 128 * j + 128, 128 * j : 128 * j + 128]
        block = jnp.where(first, part[0:E], part[E:128]).reshape(8, 8, 128)
        for half in range(2):
            c, y, slot = tile_place((moment * PAIRS + 2 * quad + j) * 8 + 4 * half)
            ref[c, y, pl.ds(slot, 4)] = block[4 * half : 4 * half + 4]


def row_place(moment, pair):
    row = moment * PAIRS + pair
    group = row // 2
    return group // YS, group % YS, row % 2


def put_row(ref, moment, pair, row):
    c, y, k = row_place(moment, pair)
    ref[c, y, TILES - 1, pl.ds(k, 1)] = row


def get_row(ref, moment, quad):
    rows = []
    for j in range(2):
        c, y, k = row_place(moment, 2 * quad + j)
        rows.append(ref[c, y, TILES - 1, pl.ds(k, 1)])
    return jnp.concatenate(rows, axis=1)


def get_blocks(ref, moment, quad, high_ref, low_ref):
    first = lax.broadcasted_iota(jnp.int32, (E, 128), 1) < E
    for j in range(2):
        halves = []
        for half in range(2):
            c, y, slot = tile_place((moment * PAIRS + 2 * quad + j) * 8 + 4 * half)
            halves.append(ref[c, y, pl.ds(slot, 4)].reshape(32, 128))
        block = jnp.concatenate(halves, axis=0)
        for k, kept in enumerate((jnp.where(first, block, 0.0), jnp.where(first, 0.0, block))):
            high, low = split(kept)
            here = pl.ds(128 * j + E * k, E), pl.ds(128 * j, 128)
            high_ref[moment, quad, here[0], here[1]] = high
            low_ref[moment, quad, here[0], here[1]] = low


class Scatter:
    def __init__(self, pos, peers, r, tag, count):
        self.pos, self.peers, self.count, self.r, self.tag = pos, peers, count, r, tag

    def ref(self, name):
        return self.r[name + self.tag]

    def put(self, name, index, result):
        xf, yf = self.ref(name + "x"), self.ref(name + "y")
        for y in range(YS):
            for x in range(XS):
                block = result[64 * y : 64 * y + 64, 128 * x : 128 * x + 128]
                xf[index, x, y] = block[0:32]
                yf[index, y, x] = block[32:64]

    def core_copies(self, index):
        s, q = self.ref("s1"), self.ref("r1")
        return [
            send(self.ref("sendx").at[index], self.ref("gotx").at[index], s.at[0, index], q.at[0, index], self.peers["c"]),
            send(self.ref("sendy").at[index], self.ref("goty").at[index], s.at[1, index], q.at[1, index], self.peers["c"]),
        ]

    def second_copies(self, index):
        x, y, _, _ = self.pos
        s, q = self.ref("s2"), self.ref("r2")
        copies = []
        for d in range(1, XS):
            copies.append(
                send(
                    self.ref("ownx").at[index, lax.rem(x + d, XS)], self.ref("bx").at[index, d - 1],
                    s.at[0, index, d - 1], q.at[0, index, d - 1], self.peers["x"][d - 1],
                )
            )
            copies.append(
                send(
                    self.ref("owny").at[index, lax.rem(y + d, YS)], self.ref("by").at[index, d - 1],
                    s.at[1, index, d - 1], q.at[1, index, d - 1], self.peers["y"][d - 1],
                )
            )
        return copies

    def start_second(self, index):
        wait(self.core_copies(index))
        for name in ("x", "y"):
            own, got = self.ref("own" + name), self.ref("got" + name)
            own[index] = own[index] + got[index]
        start(self.second_copies(index))

    def third_copies(self, index):
        x, y, _, _ = self.pos
        s, q = self.ref("s3"), self.ref("r3")
        copies = []
        for d in range(1, XS):
            copies.append(
                send(
                    self.ref("cx").at[index, lax.rem(y + d, YS)], self.ref("dx").at[index, d - 1],
                    s.at[0, index, d - 1], q.at[0, index, d - 1], self.peers["y"][d - 1],
                )
            )
            copies.append(
                send(
                    self.ref("cy").at[index, lax.rem(x + d, XS)], self.ref("dy").at[index, d - 1],
                    s.at[1, index, d - 1], q.at[1, index, d - 1], self.peers["x"][d - 1],
                )
            )
        return copies

    def start_third(self, index):
        x, y, _, _ = self.pos
        wait(self.second_copies(index))
        bx, by = self.ref("bx"), self.ref("by")
        self.ref("cx")[index] = self.ref("ownx")[index, x] + bx[index, 0] + bx[index, 1] + bx[index, 2]
        self.ref("cy")[index] = self.ref("owny")[index, y] + by[index, 0] + by[index, 1] + by[index, 2]
        start(self.third_copies(index))

    def last_copies(self):
        z = self.pos[2]
        return [
            send(
                self.ref("zs").at[lax.rem(z + d, ZS)], self.ref("zb").at[d - 1],
                self.ref("s4").at[d - 1], self.ref("r4").at[d - 1], self.peers["z"][d - 1],
            )
            for d in range(1, ZS)
        ]

    def start_last(self):
        x, y, _, _ = self.pos
        zs = self.ref("zs")
        for index in range(self.count):
            wait(self.third_copies(index))
            dx, dy = self.ref("dx"), self.ref("dy")
            low = self.ref("cx")[index, y] + dx[index, 0] + dx[index, 1] + dx[index, 2]
            high = self.ref("cy")[index, x] + dy[index, 0] + dy[index, 1] + dy[index, 2]
            zs[0:8, index] = low.reshape(8, 4, 128)
            zs[8:16, index] = high.reshape(8, 4, 128)
        start(self.last_copies())

    def finish(self, outs, scale):
        z = self.pos[2]
        wait(self.last_copies())
        zb = self.ref("zb")
        total = (self.ref("zs")[z] + sum(zb[d - 1] for d in range(1, ZS))) * scale
        for index, out in enumerate(outs):
            out[...] = total[index]


def reduce_scratch(tag):
    dma = pltpu.SemaphoreType.DMA
    return {
        "x" + tag: pltpu.VMEM((2, YS, TILES, 8, 128), F32),
        "out" + tag: pltpu.VMEM((2, YS, TILES, 8, 128), F32),
        "bufc" + tag: pltpu.VMEM((YS, TILES, 8, 128), F32),
        "accc" + tag: pltpu.VMEM((YS, TILES, 8, 128), F32),
        "bufy" + tag: pltpu.VMEM((YS - 1, TILES, 8, 128), F32),
        "accy" + tag: pltpu.VMEM((TILES, 8, 128), F32),
        "bufz" + tag: pltpu.VMEM((ZS - 1, 8, 128), F32),
        "sc" + tag: dma((2,)),
        "rc" + tag: dma((2,)),
        "sy" + tag: dma((2, YS - 1)),
        "ry" + tag: dma((2, YS - 1)),
        "sz" + tag: dma((2, ZS - 1)),
        "rz" + tag: dma((2, ZS - 1)),
    }


def scatter_scratch(tag, n):
    dma = pltpu.SemaphoreType.DMA
    names = {}
    for kind in ("send", "got", "own"):
        names[kind + "x" + tag] = pltpu.VMEM((n, XS, YS, 32, 128), F32)
        names[kind + "y" + tag] = pltpu.VMEM((n, YS, XS, 32, 128), F32)
    for axis in ("x", "y"):
        names["b" + axis + tag] = pltpu.VMEM((n, 3, 4, 32, 128), F32)
        names["c" + axis + tag] = pltpu.VMEM((n, 4, 32, 128), F32)
        names["d" + axis + tag] = pltpu.VMEM((n, 3, 32, 128), F32)
    names["zs" + tag] = pltpu.VMEM((ZS, n, 4, 128), F32)
    names["zb" + tag] = pltpu.VMEM((ZS - 1, n, 4, 128), F32)
    for k in ("1", "2", "3"):
        shape = (2, n) if k == "1" else (2, n, 3)
        names["s" + k + tag] = dma(shape)
        names["r" + k + tag] = dma(shape)
    names["s4" + tag] = dma((ZS - 1,))
    names["r4" + tag] = dma((ZS - 1,))
    return names


def scratch():
    full = pltpu.VMEM((ROWS, D), F32)
    half = pltpu.VMEM((ROWS, D), BF16)
    names = {n: full for n in ("uq", "uk", "val", "fq", "fk", "att", "rden", "gnum", "gden", "wtd", "gin")}
    names.update({n: half for n in ("fqh", "fql", "fkh", "fkl", "vh", "vl", "gnh", "gnl", "gq", "gk", "gv")})
    names["gh"] = pltpu.VMEM((ROWS, F), F32)
    names["turn"] = pltpu.VMEM((2, QUAD, ROWS), BF16)
    names["ones"] = pltpu.VMEM((QUAD, QUAD), BF16)
    names["ph"] = pltpu.VMEM((2, QUAD, QUAD), BF16)
    names["pl"] = pltpu.VMEM((2, QUAD, QUAD), BF16)
    for n in ("sh", "sl", "gsh", "gsl"):
        names[n] = pltpu.VMEM((T, 2, QUAD, QUAD), BF16)
    names.update(reduce_scratch("_1"))
    names.update(reduce_scratch("_2"))
    names.update(scatter_scratch("_q", 1))
    names.update(scatter_scratch("_kv", 2))
    return names


def kernel(
    scale, x_ref, cot_ref, wq_ref, wk_ref, wv_ref, up_ref, down_ref, proj_ref, live_ref,
    gin_ref, oq_ref, ok_ref, ov_ref, *rest,
):
    r = dict(zip(scratch().keys(), rest))
    s = lax.axis_index("sensor")
    x, y, z, c = lax.axis_index("step"), s // (2 * ZS), lax.rem(s // 2, ZS), lax.rem(s, 2)
    pos = (x, y, z, c)
    peers = {
        "c": at(x, y, z, 1 - c),
        "y": [at(x, lax.rem(y + d, YS), z, c) for d in range(1, YS)],
        "x": [at(lax.rem(x + d, XS), y, z, c) for d in range(1, XS)],
        "z": [at(x, y, lax.rem(z + d, ZS), c) for d in range(1, ZS)],
    }
    everyone = [peers["c"]] + peers["y"] + peers["x"] + peers["z"]
    barrier = pltpu.get_barrier_semaphore()
    for target in everyone:
        pl.semaphore_signal(barrier, inc=1, device_id=target, device_id_type=MESH)

    rows = x_ref[...].reshape(ROWS, D)
    row_id = lax.rem(lax.broadcasted_iota(jnp.int32, (ROWS, 1), 0), N)
    valid = row_id < live_ref[0]
    quads = [pl.ds(QUAD * q, QUAD) for q in range(2)]
    moments = [pl.ds(N * t, N) for t in range(T)]

    same = lax.broadcasted_iota(jnp.int32, (QUAD, QUAD), 0) // E == lax.broadcasted_iota(jnp.int32, (QUAD, QUAD), 1) // E
    r["ones"][...] = jnp.where(same, 1.0, 0.0).astype(BF16)
    ones = r["ones"]
    zero = jnp.zeros((E, E), F32)
    for q in range(2):
        lines = []
        for k in range(4):
            parts = [zero] * 4
            parts[k] = proj_ref[4 * q + k]
            lines.append(jnp.concatenate(parts, axis=1))
        r["ph"][q], r["pl"][q] = split(jnp.concatenate(lines, axis=0))

    def features(u_ref, q):
        u = u_ref[:, quads[q]]
        exponent = dot3(dot, split(u), (r["ph"][q], r["pl"][q])) - 0.5 * head_sum(u * u, ones[...])
        return jnp.exp(exponent) * (E ** -0.5)

    def feature_back(weighted, u, q):
        back = dot3(dot_nt, split(weighted), (r["ph"][q], r["pl"][q])) - u * head_sum(weighted, ones[...])
        return (back * FACTOR).astype(BF16)

    r["uk"][...] = dot(rows, wk_ref[...]) * FACTOR
    r["val"][...] = dot(rows, wv_ref[...])
    r["vh"][...], r["vl"][...] = split(r["val"][...])
    for q in range(2):
        fk = jnp.where(valid, features(r["uk"], q), 0.0)
        r["fk"][:, quads[q]] = fk
        r["fkh"][:, quads[q]], r["fkl"][:, quads[q]] = split(fk)

    def outer(a, b, t, q):
        (ah, al), (bh, bl) = a, b
        here = moments[t], quads[q]
        left = jnp.concatenate([ah[here], al[here], ah[here]], axis=0)
        right = jnp.concatenate([bh[here], bh[here], bl[here]], axis=0)
        return dot_tn(left, right)

    first, second = Reduce(pos, peers, r, "_1"), Reduce(pos, peers, r, "_2")
    for ref in (first.x, second.x):
        ref[:, :, TILES - 1] = jnp.zeros((2, YS, 8, 128), F32)
    for t in range(T):
        for q in range(2):
            put_blocks(first.x, t, q, outer((r["fkh"], r["fkl"]), (r["vh"], r["vl"]), t, q))
        total = jnp.sum(r["fk"][moments[t], :], axis=0, keepdims=True)
        for p in range(PAIRS):
            put_row(first.x, t, p, total[:, 128 * p : 128 * p + 128])

    pl.semaphore_wait(barrier, len(everyone))
    first.start_core()
    r["uq"][...] = dot(rows, wq_ref[...]) * FACTOR
    first.start_y()
    for q in range(2):
        fq = features(r["uq"], q)
        r["fq"][:, quads[q]] = fq
        r["fqh"][:, quads[q]], r["fql"][:, quads[q]] = split(fq)
    first.start_z()
    masked = jnp.where(valid, cot_ref[...].reshape(ROWS, D), jnp.zeros((), BF16))
    r["gh"][...] = dot_nt(masked, down_ref[...])
    for n in ("sh", "sl", "gsh", "gsl"):
        r[n][...] = jnp.zeros_like(r[n])
    first.start_z_back()
    line = lax.broadcasted_iota(jnp.int32, (QUAD, D), 0)
    column = lax.broadcasted_iota(jnp.int32, (QUAD, D), 1)
    for k in range(2):
        source = (line // 64) * 128 + lax.rem(line // 4, ZS) * 8 + 4 * k + lax.rem(line, 4)
        pick = jnp.where(source == column, 1.0, 0.0).astype(BF16)
        r["turn"][k] = dot_nt(pick, rows).astype(BF16)
    first.start_y_back()
    first.start_core_back()
    first.finish()

    for t in range(T):
        for q in range(2):
            here = moments[t], quads[q]
            get_blocks(first.out, t, q, r["sh"], r["sl"])
            numer = dot3(dot, (r["fqh"][here], r["fql"][here]), (r["sh"][t, q], r["sl"][t, q]))
            inverse = 1.0 / head_sum(r["fq"][here] * get_row(first.out, t, q), ones[...])
            r["rden"][here] = inverse
            r["att"][here] = numer * inverse
    att = r["att"][...]
    rms_inverse = 1.0 / jnp.sqrt(jnp.mean(att * att, axis=1, keepdims=True) + 1e-06)
    normed = att * rms_inverse
    pre = dot(normed.astype(BF16), up_ref[...])
    grad_pre = (r["gh"][...] * gelu_slope(pre)).astype(BF16)
    grad_normed = dot_nt(grad_pre, up_ref[...])
    mean = jnp.mean(grad_normed * normed, axis=1, keepdims=True)
    grad_att = (grad_normed - normed * mean) * rms_inverse
    for q in range(2):
        ga = grad_att[:, QUAD * q : QUAD * q + QUAD]
        inverse = r["rden"][:, quads[q]]
        gnum = ga * inverse
        r["gnum"][:, quads[q]] = gnum
        r["gnh"][:, quads[q]], r["gnl"][:, quads[q]] = split(gnum)
        r["gden"][:, quads[q]] = -head_sum(ga * r["att"][:, quads[q]], ones[...]) * inverse
    for t in range(T):
        for q in range(2):
            put_blocks(second.x, t, q, outer((r["fqh"], r["fql"]), (r["gnh"], r["gnl"]), t, q))
        total = jnp.sum(r["fq"][moments[t], :] * r["gden"][moments[t], :], axis=0, keepdims=True)
        for p in range(PAIRS):
            put_row(second.x, t, p, total[:, 128 * p : 128 * p + 128])

    second.start_core()
    for t in range(T):
        for q in range(2):
            here = moments[t], quads[q]
            gfq = dot3(dot_nt, (r["gnh"][here], r["gnl"][here]), (r["sh"][t, q], r["sl"][t, q]))
            gfq = gfq + r["gden"][here] * get_row(first.out, t, q)
            r["wtd"][here] = gfq * r["fq"][here]
    second.start_y()
    for q in range(2):
        r["gq"][:, quads[q]] = feature_back(r["wtd"][:, quads[q]], r["uq"][:, quads[q]], q)
    job_q, job_kv = Scatter(pos, peers, r, "_q", 1), Scatter(pos, peers, r, "_kv", 2)
    job_q.put("send", 0, dot(r["turn"][1 - c], r["gq"][...]))
    second.start_z()
    start(job_q.core_copies(0))
    job_q.put("own", 0, dot(r["turn"][c], r["gq"][...]))
    job_q.start_second(0)
    r["gin"][...] = dot_nt(r["gq"][...], wq_ref[...])
    second.start_z_back()
    job_q.start_third(0)
    second.start_y_back()
    second.start_core_back()
    job_q.start_last()
    second.finish()

    for t in range(T):
        for q in range(2):
            here = moments[t], quads[q]
            get_blocks(second.out, t, q, r["gsh"], r["gsl"])
            blocks = (r["gsh"][t, q], r["gsl"][t, q])
            r["gv"][here] = dot3(dot, (r["fkh"][here], r["fkl"][here]), blocks).astype(BF16)
    job_kv.put("send", 1, dot(r["turn"][1 - c], r["gv"][...]))
    start(job_kv.core_copies(1))
    for t in range(T):
        for q in range(2):
            here = moments[t], quads[q]
            blocks = (r["gsh"][t, q], r["gsl"][t, q])
            gfk = dot3(dot_nt, (r["vh"][here], r["vl"][here]), blocks) + get_row(second.out, t, q)
            r["wtd"][here] = gfk * r["fk"][here]
    for q in range(2):
        r["gk"][:, quads[q]] = feature_back(r["wtd"][:, quads[q]], r["uk"][:, quads[q]], q)
    job_kv.put("send", 0, dot(r["turn"][1 - c], r["gk"][...]))
    start(job_kv.core_copies(0))
    job_kv.put("own", 1, dot(r["turn"][c], r["gv"][...]))
    job_kv.start_second(1)
    job_kv.put("own", 0, dot(r["turn"][c], r["gk"][...]))
    job_kv.start_second(0)
    total = r["gin"][...] + dot_nt(r["gk"][...], wk_ref[...]) + dot_nt(r["gv"][...], wv_ref[...])
    gin_ref[...] = total.astype(BF16).reshape(T, N, D)
    job_q.finish((oq_ref,), scale)
    job_kv.start_third(1)
    job_kv.start_third(0)
    job_kv.start_last()
    job_kv.finish((ok_ref, ov_ref), scale)
    first.drain()
    second.drain()


def shards(inputs, cotangent, w_query, w_key, w_value, w_up, w_down, feature_proj, live_count):
    total_rows = T * XS * N * YS * ZS * 2
    piece = jax.ShapeDtypeStruct((4, 128), F32)
    return pl.pallas_call(
        functools.partial(kernel, 1.0 / math.sqrt(total_rows)),
        out_shape=(jax.ShapeDtypeStruct((T, N, D), BF16), piece, piece, piece),
        in_specs=[VM] * 8 + [SM],
        out_specs=(VM,) * 4,
        scratch_shapes=list(scratch().values()),
        compiler_params=pltpu.CompilerParams(collective_id=0, has_side_effects=True, vmem_limit_bytes=56 << 20),
    )(inputs, cotangent, w_query, w_key, w_value, w_up, w_down, feature_proj, live_count)


def solution(mesh):
    placed = (P("step", "sensor", None),) * 2 + (P(),) * 6 + (P("sensor"),)
    return jax.shard_map(
        shards,
        mesh=mesh,
        in_specs=placed,
        out_specs=(P("step", "sensor", None),) + (P("sensor", "step"),) * 3,
        check_vma=False,
    )
```

```python
import functools
import math

import jax
import jax.numpy as jnp
from jax import lax
from jax.experimental import pallas as pl
from jax.experimental.pallas import tpu as pltpu
from jax.sharding import PartitionSpec as P

MESH = pl.DeviceIdType.MESH
VM = pl.BlockSpec(memory_space=pltpu.VMEM)
ANY = pl.BlockSpec(memory_space=pl.ANY)
F32, BF16 = jnp.float32, jnp.bfloat16
YS, ZS, XS = 4, 16, 4
T, N, D, F, H, E = 3, 64, 512, 256, 8, 64
ROWS = T * N
PAIRS = H // 2
TILES = 13
QUAD = 256
FACTOR = E ** (-0.25)
STAGED = {
    "x": ((T, N, D), BF16),
    "wk": ((D, D), BF16),
    "proj": ((H, E, E), F32),
    "wv": ((D, D), BF16),
    "live": ((1,), jnp.int32),
    "wq": ((D, D), BF16),
    "cot": ((T, N, D), BF16),
    "down": ((F, D), BF16),
    "up": ((D, F), BF16),
}
FAR_4 = (2, 1, 3)
FAR_16 = (8, 7, 9, 6, 10, 5, 11, 4, 12, 3, 13, 2, 14, 1, 15)


def at(x, y, z, c):
    return ((y * ZS + z) * 2 + c, x)


def send(src, dst, ssem, rsem, target):
    return pltpu.make_async_remote_copy(
        src_ref=src, dst_ref=dst, send_sem=ssem, recv_sem=rsem, device_id=target, device_id_type=MESH
    )


def start(copies):
    for copy in copies:
        copy.start()


def wait(copies):
    for copy in copies:
        copy.wait()


def dot(a, b):
    return lax.dot_general(a, b, (((1,), (0,)), ((), ())), preferred_element_type=F32)


def dot_nt(a, b):
    return lax.dot_general(a, b, (((1,), (1,)), ((), ())), preferred_element_type=F32)


def dot_tn(a, b):
    return lax.dot_general(a, b, (((0,), (0,)), ((), ())), preferred_element_type=F32)


def split(value):
    high = value.astype(BF16)
    return high, (value - high.astype(F32)).astype(BF16)


def dot3(product, a, b):
    return product(a[0], b[0]) + product(a[1], b[0]) + product(a[0], b[1])


def head_sum(value, ones):
    high, low = split(value)
    return dot(high, ones) + dot(low, ones)


def gelu_slope(v):
    k = math.sqrt(2 / math.pi)
    th = jnp.tanh(k * (v + 0.044715 * v * v * v))
    return 0.5 * (1.0 + th) + 0.5 * v * (1.0 - th * th) * (k * (1.0 + 3 * 0.044715 * v * v))


class Reduce:
    def __init__(self, pos, peers, r, tag):
        self.pos, self.peers = pos, peers
        self.x, self.out = r["x" + tag], r["out" + tag]
        self.buf_c, self.acc_c = r["bufc" + tag], r["accc" + tag]
        self.buf_y, self.acc_y, self.buf_z = r["bufy" + tag], r["accy" + tag], r["bufz" + tag]
        self.sc, self.rc, self.sy, self.ry = r["sc" + tag], r["rc" + tag], r["sy" + tag], r["ry" + tag]
        self.sz, self.rz = r["sz" + tag], r["rz" + tag]

    def core_down(self, k):
        chunk = lax.rem(self.pos[1] + k, YS)
        return send(
            self.x.at[1 - self.pos[3], chunk], self.buf_c.at[chunk], self.sc.at[0, k], self.rc.at[0, k], self.peers["c"]
        )

    def y_down(self, d):
        chunk = lax.rem(self.pos[1] + d, YS)
        return send(
            self.acc_c.at[chunk], self.buf_y.at[d - 1], self.sy.at[0, d - 1], self.ry.at[0, d - 1],
            self.peers["y"][d - 1],
        )

    def z_down(self, d, slot):
        return send(
            self.acc_y.at[slot], self.buf_z.at[d - 1], self.sz.at[0, d - 1], self.rz.at[0, d - 1], self.peers["z"][d - 1]
        )

    def z_up(self, d, slot):
        piece = self.out.at[self.pos[3], self.pos[1], slot]
        return send(piece, piece, self.sz.at[1, d - 1], self.rz.at[1, d - 1], self.peers["z"][d - 1])

    def y_up(self, d, piece):
        return send(piece, piece, self.sy.at[1, d - 1], self.ry.at[1, d - 1], self.peers["y"][d - 1])

    def core_up(self, k, group):
        piece = self.out.at[self.pos[3], group]
        return send(piece, piece, self.sc.at[1, k], self.rc.at[1, k], self.peers["c"])

    def start_core(self):
        for k in FAR_4 + (0,):
            self.core_down(k).start()

    def start_y(self):
        _, y, _, c = self.pos
        for k in FAR_4 + (0,):
            self.core_down(k).wait()
            chunk = lax.rem(y + k, YS)
            self.acc_c[chunk] = self.x[c, chunk] + self.buf_c[chunk]
            if k:
                self.y_down(k).start()

    def start_z(self):
        _, y, z, _ = self.pos
        for d in range(1, YS):
            self.y_down(d).wait()
        self.acc_y[...] = self.acc_c[y] + self.buf_y[0] + self.buf_y[1] + self.buf_y[2]
        for d in FAR_16:
            other = lax.rem(z + d, ZS)

            @pl.when(other < TILES)
            def _():
                self.z_down(d, other).start()

    def start_z_back(self):
        _, y, z, c = self.pos

        @pl.when(z < TILES)
        def _():
            for d in range(1, ZS):
                self.z_down(d, 0).wait_recv()
            self.out[c, y, z] = self.acc_y[z] + sum(self.buf_z[d - 1] for d in range(1, ZS))
            for d in FAR_16:
                self.z_up(d, z).start()
            for d in FAR_4:
                self.y_up(d, self.out.at[c, y, z]).start()

    def start_y_back(self):
        _, y, z, c = self.pos
        for d in FAR_16[::-1]:
            source = lax.rem(z + ZS - d, ZS)

            @pl.when(source < TILES)
            def _():
                self.z_up(d, source).wait_recv()
                for e in FAR_4:
                    self.y_up(e, self.out.at[c, y, source]).start()

    def start_core_back(self):
        _, y, _, c = self.pos
        self.core_up(0, y).start()
        for d in (1, 3, 2):
            group = lax.rem(y + YS - d, YS)
            self.y_up(d, self.out.at[c, group]).wait_recv()
            self.core_up(d, group).start()

    def finish(self):
        for k in range(YS):
            group = lax.rem(self.pos[1] + YS - k, YS)
            piece = self.out.at[1 - self.pos[3], group]
            send(piece, piece, self.sc.at[1, k], self.rc.at[1, k], self.peers["c"]).wait_recv()

    def drain(self):
        _, y, z, c = self.pos
        for d in range(1, ZS):
            other = lax.rem(z + d, ZS)

            @pl.when(other < TILES)
            def _():
                self.z_down(d, other).wait_send()

        @pl.when(z < TILES)
        def _():
            for d in range(1, ZS):
                self.z_up(d, z).wait_send()

        for d in range(1, YS):
            self.y_up(d, self.out.at[c, y]).wait_send()
        for k in range(YS):
            self.core_up(k, lax.rem(y + YS - k, YS)).wait_send()


def tile_place(tile):
    group, slot = divmod(tile, 12)
    return group // YS, group % YS, slot


def put_blocks(ref, moment, quad, result):
    first = lax.broadcasted_iota(jnp.int32, (E, 128), 1) < E
    for j in range(2):
        part = result[128 * j : 128 * j + 128, 128 * j : 128 * j + 128]
        block = jnp.where(first, part[0:E], part[E:128]).reshape(8, 8, 128)
        for half in range(2):
            c, y, slot = tile_place((moment * PAIRS + 2 * quad + j) * 8 + 4 * half)
            ref[c, y, pl.ds(slot, 4)] = block[4 * half : 4 * half + 4]


def row_place(moment, pair):
    row = moment * PAIRS + pair
    group = row // 2
    return group // YS, group % YS, row % 2


def put_row(ref, moment, pair, row):
    c, y, k = row_place(moment, pair)
    ref[c, y, TILES - 1, pl.ds(k, 1)] = row


def get_row(ref, moment, quad):
    rows = []
    for j in range(2):
        c, y, k = row_place(moment, 2 * quad + j)
        rows.append(ref[c, y, TILES - 1, pl.ds(k, 1)])
    return jnp.concatenate(rows, axis=1)


def get_blocks(ref, moment, quad, high_ref, low_ref):
    first = lax.broadcasted_iota(jnp.int32, (E, 128), 1) < E
    for j in range(2):
        halves = []
        for half in range(2):
            c, y, slot = tile_place((moment * PAIRS + 2 * quad + j) * 8 + 4 * half)
            halves.append(ref[c, y, pl.ds(slot, 4)].reshape(32, 128))
        block = jnp.concatenate(halves, axis=0)
        for k, kept in enumerate((jnp.where(first, block, 0.0), jnp.where(first, 0.0, block))):
            high, low = split(kept)
            here = pl.ds(128 * j + E * k, E), pl.ds(128 * j, 128)
            high_ref[moment, quad, here[0], here[1]] = high
            low_ref[moment, quad, here[0], here[1]] = low


class Scatter:
    def __init__(self, pos, peers, r, tag):
        self.pos, self.peers, self.r, self.tag = pos, peers, r, tag

    def ref(self, name):
        return self.r[name + self.tag]

    def put(self, name, result):
        xf, yf = self.ref(name + "x"), self.ref(name + "y")
        for y in range(YS):
            for x in range(XS):
                block = result[64 * y : 64 * y + 64, 128 * x : 128 * x + 128]
                xf[x, y] = block[0:32]
                yf[y, x] = block[32:64]

    def sems(self, phase, half, k):
        return self.ref("s" + phase).at[half, k], self.ref("r" + phase).at[half, k]

    def chunk(self, half, k):
        return lax.rem(self.pos[half] + k, 4)

    def core_copy(self, half, k):
        name, chunk = "xy"[half], self.chunk(half, k)
        return send(
            self.ref("send" + name).at[chunk], self.ref("got" + name).at[chunk], *self.sems("1", half, k), self.peers["c"]
        )

    def second_copy(self, half, d):
        name = "xy"[half]
        return send(
            self.ref("own" + name).at[self.chunk(half, d)], self.ref("b" + name).at[d - 1],
            *self.sems("2", half, d - 1), self.peers[name][d - 1],
        )

    def third_copy(self, half, d):
        name, other = "xy"[half], "yx"[half]
        return send(
            self.ref("c" + name).at[self.chunk(1 - half, d)], self.ref("d" + name).at[d - 1],
            *self.sems("3", half, d - 1), self.peers[other][d - 1],
        )

    def last_copy(self, d):
        return send(
            self.ref("zs").at[lax.rem(self.pos[2] + d, ZS)], self.ref("zb").at[d - 1],
            self.ref("s4").at[d - 1], self.ref("r4").at[d - 1], self.peers["z"][d - 1],
        )

    def start_core(self):
        for k in FAR_4 + (0,):
            for half in range(2):
                self.core_copy(half, k).start()

    def start_second(self):
        for k in FAR_4 + (0,):
            for half in range(2):
                self.core_copy(half, k).wait()
                own, got = self.ref("own" + "xy"[half]), self.ref("got" + "xy"[half])
                chunk = self.chunk(half, k)
                own[chunk] = own[chunk] + got[chunk]
                if k:
                    self.second_copy(half, k).start()

    def start_third(self):
        for half in range(2):
            name = "xy"[half]
            for d in range(1, 4):
                self.second_copy(half, d).wait()
            got = self.ref("b" + name)
            self.ref("c" + name)[...] = self.ref("own" + name)[self.pos[half]] + got[0] + got[1] + got[2]
            for d in FAR_4:
                self.third_copy(half, d).start()

    def start_last(self):
        zs = self.ref("zs")
        for half in range(2):
            for d in range(1, 4):
                self.third_copy(half, d).wait()
            got = self.ref("d" + "xy"[half])
            total = self.ref("c" + "xy"[half])[self.pos[1 - half]] + got[0] + got[1] + got[2]
            zs[8 * half : 8 * half + 8] = total.reshape(8, 4, 128)
        for d in FAR_16:
            self.last_copy(d).start()

    def finish(self, out, scale):
        for d in range(1, ZS):
            self.last_copy(d).wait()
        zb = self.ref("zb")
        out[...] = (self.ref("zs")[self.pos[2]] + sum(zb[d - 1] for d in range(1, ZS))) * scale


def reduce_scratch(tag):
    dma = pltpu.SemaphoreType.DMA
    return {
        "x" + tag: pltpu.VMEM((2, YS, TILES, 8, 128), F32),
        "out" + tag: pltpu.VMEM((2, YS, TILES, 8, 128), F32),
        "bufc" + tag: pltpu.VMEM((YS, TILES, 8, 128), F32),
        "accc" + tag: pltpu.VMEM((YS, TILES, 8, 128), F32),
        "bufy" + tag: pltpu.VMEM((YS - 1, TILES, 8, 128), F32),
        "accy" + tag: pltpu.VMEM((TILES, 8, 128), F32),
        "bufz" + tag: pltpu.VMEM((ZS - 1, 8, 128), F32),
        "sc" + tag: dma((2, YS)),
        "rc" + tag: dma((2, YS)),
        "sy" + tag: dma((2, YS - 1)),
        "ry" + tag: dma((2, YS - 1)),
        "sz" + tag: dma((2, ZS - 1)),
        "rz" + tag: dma((2, ZS - 1)),
    }


def scatter_scratch(tag):
    dma = pltpu.SemaphoreType.DMA
    names = {}
    for axis in ("x", "y"):
        for kind in ("send", "got", "own"):
            names[kind + axis + tag] = pltpu.VMEM((4, 4, 32, 128), F32)
        names["b" + axis + tag] = pltpu.VMEM((3, 4, 32, 128), F32)
        names["c" + axis + tag] = pltpu.VMEM((4, 32, 128), F32)
        names["d" + axis + tag] = pltpu.VMEM((3, 32, 128), F32)
    names["zs" + tag] = pltpu.VMEM((ZS, 4, 128), F32)
    names["zb" + tag] = pltpu.VMEM((ZS - 1, 4, 128), F32)
    for k in ("1", "2", "3"):
        names["s" + k + tag] = dma((2, 4))
        names["r" + k + tag] = dma((2, 4))
    names["s4" + tag] = dma((ZS - 1,))
    names["r4" + tag] = dma((ZS - 1,))
    return names


def scratch():
    full = pltpu.VMEM((ROWS, D), F32)
    half = pltpu.VMEM((ROWS, D), BF16)
    names = {n: full for n in ("uq", "uk", "fq", "fk", "att", "rden", "gnum", "gden", "wtd", "gin")}
    names.update({n: half for n in ("fqh", "fql", "fkh", "fkl", "vh", "vl", "gnh", "gnl", "gq", "gk", "gv")})
    names["gh"] = pltpu.VMEM((ROWS, F), F32)
    names["turn"] = pltpu.VMEM((2, QUAD, ROWS), BF16)
    names["ones"] = pltpu.VMEM((QUAD, QUAD), BF16)
    names["ph"] = pltpu.VMEM((2, QUAD, QUAD), BF16)
    names["pl"] = pltpu.VMEM((2, QUAD, QUAD), BF16)
    for n in ("sh", "sl", "gsh", "gsl"):
        names[n] = pltpu.VMEM((T, 2, QUAD, QUAD), BF16)
    names.update(reduce_scratch("_1"))
    names.update(reduce_scratch("_2"))
    for tag in ("_q", "_k", "_v"):
        names.update(scatter_scratch(tag))
    for n, (shape, kind) in STAGED.items():
        names["in_" + n] = pltpu.SMEM(shape, kind) if n == "live" else pltpu.VMEM(shape, kind)
    names["fetch"] = pltpu.SemaphoreType.DMA((len(STAGED),))
    return names


def kernel(
    scale, x_hbm, cot_hbm, wq_hbm, wk_hbm, wv_hbm, up_hbm, down_hbm, proj_hbm, live_hbm,
    gin_ref, oq_ref, ok_ref, ov_ref, *rest,
):
    r = dict(zip(scratch().keys(), rest))
    sources = dict(
        x=x_hbm, cot=cot_hbm, wq=wq_hbm, wk=wk_hbm, wv=wv_hbm, up=up_hbm, down=down_hbm, proj=proj_hbm, live=live_hbm
    )
    fetches = {
        n: pltpu.make_async_copy(sources[n], r["in_" + n], r["fetch"].at[i]) for i, n in enumerate(STAGED)
    }
    start(fetches.values())

    def fetched(n):
        fetches[n].wait()
        return r["in_" + n]

    s = lax.axis_index("sensor")
    x, y, z, c = lax.axis_index("step"), s // (2 * ZS), lax.rem(s // 2, ZS), lax.rem(s, 2)
    pos = (x, y, z, c)
    peers = {
        "c": at(x, y, z, 1 - c),
        "y": [at(x, lax.rem(y + d, YS), z, c) for d in range(1, YS)],
        "x": [at(lax.rem(x + d, XS), y, z, c) for d in range(1, XS)],
        "z": [at(x, y, lax.rem(z + d, ZS), c) for d in range(1, ZS)],
    }
    everyone = [peers["c"]] + peers["y"] + peers["x"] + peers["z"]
    barrier = pltpu.get_barrier_semaphore()
    for target in everyone:
        pl.semaphore_signal(barrier, inc=1, device_id=target, device_id_type=MESH)

    row_id = lax.rem(lax.broadcasted_iota(jnp.int32, (ROWS, 1), 0), N)
    quads = [pl.ds(QUAD * q, QUAD) for q in range(2)]
    moments = [pl.ds(N * t, N) for t in range(T)]

    same = lax.broadcasted_iota(jnp.int32, (QUAD, QUAD), 0) // E == lax.broadcasted_iota(jnp.int32, (QUAD, QUAD), 1) // E
    r["ones"][...] = jnp.where(same, 1.0, 0.0).astype(BF16)
    ones = r["ones"]
    zero = jnp.zeros((E, E), F32)
    rows = fetched("x")[...].reshape(ROWS, D)
    r["uk"][...] = dot(rows, fetched("wk")[...]) * FACTOR
    proj_ref = fetched("proj")
    for q in range(2):
        lines = []
        for k in range(4):
            parts = [zero] * 4
            parts[k] = proj_ref[4 * q + k]
            lines.append(jnp.concatenate(parts, axis=1))
        r["ph"][q], r["pl"][q] = split(jnp.concatenate(lines, axis=0))

    def features(u_ref, q):
        u = u_ref[:, quads[q]]
        exponent = dot3(dot, split(u), (r["ph"][q], r["pl"][q])) - 0.5 * head_sum(u * u, ones[...])
        return jnp.exp(exponent) * (E ** -0.5)

    def feature_back(weighted, u, q):
        back = dot3(dot_nt, split(weighted), (r["ph"][q], r["pl"][q])) - u * head_sum(weighted, ones[...])
        return (back * FACTOR).astype(BF16)

    r["vh"][...], r["vl"][...] = split(dot(rows, fetched("wv")[...]))
    valid = row_id < fetched("live")[0]
    for q in range(2):
        fk = jnp.where(valid, features(r["uk"], q), 0.0)
        r["fk"][:, quads[q]] = fk
        r["fkh"][:, quads[q]], r["fkl"][:, quads[q]] = split(fk)

    def outer(a, b, t, q):
        (ah, al), (bh, bl) = a, b
        here = moments[t], quads[q]
        left = jnp.concatenate([ah[here], al[here], ah[here]], axis=0)
        right = jnp.concatenate([bh[here], bh[here], bl[here]], axis=0)
        return dot_tn(left, right)

    first, second = Reduce(pos, peers, r, "_1"), Reduce(pos, peers, r, "_2")
    for ref in (first.x, second.x):
        ref[:, :, TILES - 1] = jnp.zeros((2, YS, 8, 128), F32)
    for t in range(T):
        for q in range(2):
            put_blocks(first.x, t, q, outer((r["fkh"], r["fkl"]), (r["vh"], r["vl"]), t, q))
        total = jnp.sum(r["fk"][moments[t], :], axis=0, keepdims=True)
        for p in range(PAIRS):
            put_row(first.x, t, p, total[:, 128 * p : 128 * p + 128])

    pl.semaphore_wait(barrier, len(everyone))
    first.start_core()
    wq_ref = fetched("wq")
    r["uq"][...] = dot(rows, wq_ref[...]) * FACTOR
    first.start_y()
    for q in range(2):
        fq = features(r["uq"], q)
        r["fq"][:, quads[q]] = fq
        r["fqh"][:, quads[q]], r["fql"][:, quads[q]] = split(fq)
    first.start_z()
    masked = jnp.where(valid, fetched("cot")[...].reshape(ROWS, D), jnp.zeros((), BF16))
    r["gh"][...] = dot_nt(masked, fetched("down")[...])
    up_ref = fetched("up")
    for n in ("sh", "sl", "gsh", "gsl"):
        r[n][...] = jnp.zeros_like(r[n])
    first.start_z_back()
    line = lax.broadcasted_iota(jnp.int32, (QUAD, D), 0)
    column = lax.broadcasted_iota(jnp.int32, (QUAD, D), 1)
    for k in range(2):
        source = (line // 64) * 128 + lax.rem(line // 4, ZS) * 8 + 4 * k + lax.rem(line, 4)
        pick = jnp.where(source == column, 1.0, 0.0).astype(BF16)
        r["turn"][k] = dot_nt(pick, rows).astype(BF16)
    first.start_y_back()
    first.start_core_back()
    first.finish()

    for t in range(T):
        for q in range(2):
            here = moments[t], quads[q]
            get_blocks(first.out, t, q, r["sh"], r["sl"])
            numer = dot3(dot, (r["fqh"][here], r["fql"][here]), (r["sh"][t, q], r["sl"][t, q]))
            inverse = 1.0 / head_sum(r["fq"][here] * get_row(first.out, t, q), ones[...])
            r["rden"][here] = inverse
            r["att"][here] = numer * inverse
    att = r["att"][...]
    rms_inverse = 1.0 / jnp.sqrt(jnp.mean(att * att, axis=1, keepdims=True) + 1e-06)
    normed = att * rms_inverse
    pre = dot(normed.astype(BF16), up_ref[...])
    grad_pre = (r["gh"][...] * gelu_slope(pre)).astype(BF16)
    grad_normed = dot_nt(grad_pre, up_ref[...])
    mean = jnp.mean(grad_normed * normed, axis=1, keepdims=True)
    grad_att = (grad_normed - normed * mean) * rms_inverse
    for q in range(2):
        ga = grad_att[:, QUAD * q : QUAD * q + QUAD]
        inverse = r["rden"][:, quads[q]]
        gnum = ga * inverse
        r["gnum"][:, quads[q]] = gnum
        r["gnh"][:, quads[q]], r["gnl"][:, quads[q]] = split(gnum)
        r["gden"][:, quads[q]] = -head_sum(ga * r["att"][:, quads[q]], ones[...]) * inverse
    for t in range(T):
        for q in range(2):
            put_blocks(second.x, t, q, outer((r["fqh"], r["fql"]), (r["gnh"], r["gnl"]), t, q))
        total = jnp.sum(r["fq"][moments[t], :] * r["gden"][moments[t], :], axis=0, keepdims=True)
        for p in range(PAIRS):
            put_row(second.x, t, p, total[:, 128 * p : 128 * p + 128])

    second.start_core()
    for t in range(T):
        for q in range(2):
            here = moments[t], quads[q]
            gfq = dot3(dot_nt, (r["gnh"][here], r["gnl"][here]), (r["sh"][t, q], r["sl"][t, q]))
            gfq = gfq + r["gden"][here] * get_row(first.out, t, q)
            r["wtd"][here] = gfq * r["fq"][here]
    second.start_y()
    for q in range(2):
        r["gq"][:, quads[q]] = feature_back(r["wtd"][:, quads[q]], r["uq"][:, quads[q]], q)
    job_q, job_k, job_v = (Scatter(pos, peers, r, tag) for tag in ("_q", "_k", "_v"))
    job_q.put("send", dot(r["turn"][1 - c], r["gq"][...]))
    second.start_z()
    job_q.start_core()
    job_q.put("own", dot(r["turn"][c], r["gq"][...]))
    job_q.start_second()
    r["gin"][...] = dot_nt(r["gq"][...], wq_ref[...])
    second.start_z_back()
    job_q.start_third()
    second.start_y_back()
    second.start_core_back()
    job_q.start_last()
    second.finish()

    for t in range(T):
        for q in range(2):
            here = moments[t], quads[q]
            get_blocks(second.out, t, q, r["gsh"], r["gsl"])
            blocks = (r["gsh"][t, q], r["gsl"][t, q])
            r["gv"][here] = dot3(dot, (r["fkh"][here], r["fkl"][here]), blocks).astype(BF16)
    job_v.put("send", dot(r["turn"][1 - c], r["gv"][...]))
    job_v.start_core()
    for t in range(T):
        for q in range(2):
            here = moments[t], quads[q]
            blocks = (r["gsh"][t, q], r["gsl"][t, q])
            gfk = dot3(dot_nt, (r["vh"][here], r["vl"][here]), blocks) + get_row(second.out, t, q)
            r["wtd"][here] = gfk * r["fk"][here]
    for q in range(2):
        r["gk"][:, quads[q]] = feature_back(r["wtd"][:, quads[q]], r["uk"][:, quads[q]], q)
    job_k.put("send", dot(r["turn"][1 - c], r["gk"][...]))
    job_k.start_core()
    job_v.put("own", dot(r["turn"][c], r["gv"][...]))
    job_v.start_second()
    job_k.put("own", dot(r["turn"][c], r["gk"][...]))
    job_k.start_second()
    total = r["gin"][...] + dot_nt(r["gk"][...], r["in_wk"][...]) + dot_nt(r["gv"][...], r["in_wv"][...])
    gin_ref[...] = total.astype(BF16).reshape(T, N, D)
    job_v.start_third()
    job_k.start_third()
    job_v.start_last()
    job_k.start_last()
    job_q.finish(oq_ref, scale)
    job_v.finish(ov_ref, scale)
    job_k.finish(ok_ref, scale)
    first.drain()
    second.drain()


def hand_on(*refs):
    ins, outs, sem = refs[:4], refs[4:8], refs[8]
    copies = [pltpu.make_async_copy(a, b, sem.at[i]) for i, (a, b) in enumerate(zip(ins, outs))]
    start(copies)
    wait(copies)


def shards(inputs, cotangent, w_query, w_key, w_value, w_up, w_down, feature_proj, live_count):
    total_rows = T * XS * N * YS * ZS * 2
    piece = jax.ShapeDtypeStruct((4, 128), F32)
    shapes = (jax.ShapeDtypeStruct((T, N, D), BF16), piece, piece, piece)
    results = pl.pallas_call(
        functools.partial(kernel, 1.0 / math.sqrt(total_rows)),
        out_shape=shapes,
        in_specs=[ANY] * 8 + [pl.BlockSpec(memory_space=pltpu.HBM)],
        out_specs=(VM,) * 4,
        scratch_shapes=list(scratch().values()),
        compiler_params=pltpu.CompilerParams(collective_id=0, has_side_effects=True, vmem_limit_bytes=56 << 20),
    )(inputs, cotangent, w_query, w_key, w_value, w_up, w_down, feature_proj, live_count)
    return pl.pallas_call(
        hand_on,
        out_shape=shapes,
        in_specs=[ANY] * 4,
        out_specs=(ANY,) * 4,
        scratch_shapes=[pltpu.SemaphoreType.DMA((4,))],
    )(*results)


def solution(mesh):
    placed = (P("step", "sensor", None),) * 2 + (P(),) * 6 + (P("sensor"),)
    return jax.shard_map(
        shards,
        mesh=mesh,
        in_specs=placed,
        out_specs=(P("step", "sensor", None),) + (P("sensor", "step"),) * 3,
        check_vma=False,
    )
```

```python
import functools
import math

import jax
import jax.numpy as jnp
from jax import lax
from jax.experimental import pallas as pl
from jax.experimental.pallas import tpu as pltpu
from jax.sharding import PartitionSpec as P

MESH = pl.DeviceIdType.MESH
VM = pl.BlockSpec(memory_space=pltpu.VMEM)
SM = pl.BlockSpec(memory_space=pltpu.SMEM)
ANY = pl.BlockSpec(memory_space=pl.ANY)
F32, BF16 = jnp.float32, jnp.bfloat16
YS, ZS, XS = 4, 16, 4
T, N, D, F, H, E = 3, 64, 512, 256, 8, 64
ROWS = T * N
PAIRS = H // 2
TILES = 13
QUAD = 256
FACTOR = E ** (-0.25)
STAGED = {
    "x": ((T, N, D), BF16),
    "wk": ((D, D), BF16),
    "proj": ((H, E, E), F32),
    "wv": ((D, D), BF16),
    "wq": ((D, D), BF16),
    "cot": ((T, N, D), BF16),
    "down": ((F, D), BF16),
    "up": ((D, F), BF16),
}
FAR_4 = (2, 1, 3)
FAR_16 = (8, 7, 9, 6, 10, 5, 11, 4, 12, 3, 13, 2, 14, 1, 15)


def at(x, y, z, c):
    return ((y * ZS + z) * 2 + c, x)


def send(src, dst, ssem, rsem, target):
    return pltpu.make_async_remote_copy(
        src_ref=src, dst_ref=dst, send_sem=ssem, recv_sem=rsem, device_id=target, device_id_type=MESH
    )


def start(copies):
    for copy in copies:
        copy.start()


def wait(copies):
    for copy in copies:
        copy.wait()


def dot(a, b):
    return lax.dot_general(a, b, (((1,), (0,)), ((), ())), preferred_element_type=F32)


def dot_nt(a, b):
    return lax.dot_general(a, b, (((1,), (1,)), ((), ())), preferred_element_type=F32)


def dot_tn(a, b):
    return lax.dot_general(a, b, (((0,), (0,)), ((), ())), preferred_element_type=F32)


def split(value):
    high = value.astype(BF16)
    return high, (value - high.astype(F32)).astype(BF16)


def dot3(product, a, b):
    return product(a[0], b[0]) + product(a[1], b[0]) + product(a[0], b[1])


def head_sum(value, ones):
    high, low = split(value)
    return dot(high, ones) + dot(low, ones)


def gelu_slope(v):
    k = math.sqrt(2 / math.pi)
    th = jnp.tanh(k * (v + 0.044715 * v * v * v))
    return 0.5 * (1.0 + th) + 0.5 * v * (1.0 - th * th) * (k * (1.0 + 3 * 0.044715 * v * v))


class Reduce:
    def __init__(self, pos, peers, r, tag):
        self.pos, self.peers = pos, peers
        self.x, self.out = r["x" + tag], r["out" + tag]
        self.buf_c, self.acc_c = r["bufc" + tag], r["accc" + tag]
        self.buf_y, self.acc_y, self.buf_z = r["bufy" + tag], r["accy" + tag], r["bufz" + tag]
        self.sc, self.rc, self.sy, self.ry = r["sc" + tag], r["rc" + tag], r["sy" + tag], r["ry" + tag]
        self.sz, self.rz, self.ryd = r["sz" + tag], r["rz" + tag], r["ryd" + tag]

    def core_down(self, k):
        chunk = lax.rem(self.pos[1] + k, YS)
        return send(
            self.x.at[1 - self.pos[3], chunk], self.buf_c.at[chunk], self.sc.at[0, k], self.rc.at[0, k], self.peers["c"]
        )

    def y_down(self, d, tiles):
        chunk = lax.rem(self.pos[1] + d, YS)
        if tiles is None:
            source, target, arrived = self.acc_c.at[chunk], self.buf_y.at[d - 1], self.ryd.at[d - 1, 0]
        else:
            source, target = self.acc_c.at[chunk, tiles], self.buf_y.at[d - 1, tiles]
            arrived = self.ryd.at[d - 1, tiles]
        return send(source, target, self.sy.at[0, d - 1], arrived, self.peers["y"][d - 1])

    def z_down(self, d, slot):
        return send(
            self.acc_y.at[slot], self.buf_z.at[d - 1], self.sz.at[0, d - 1], self.rz.at[0, d - 1], self.peers["z"][d - 1]
        )

    def z_up(self, d, slot):
        piece = self.out.at[self.pos[3], self.pos[1], slot]
        return send(piece, piece, self.sz.at[1, d - 1], self.rz.at[1, d - 1], self.peers["z"][d - 1])

    def y_up(self, d, piece):
        return send(piece, piece, self.sy.at[1, d - 1], self.ry.at[1, d - 1], self.peers["y"][d - 1])

    def core_up(self, k, group):
        piece = self.out.at[self.pos[3], group]
        return send(piece, piece, self.sc.at[1, k], self.rc.at[1, k], self.peers["c"])

    def start_core(self):
        for k in FAR_4 + (0,):
            self.core_down(k).start()

    def start_y(self):
        _, y, z, c = self.pos
        for k in FAR_4 + (0,):
            self.core_down(k).wait()
            chunk = lax.rem(y + k, YS)
            self.acc_c[chunk] = self.x[c, chunk] + self.buf_c[chunk]
            if k:
                for d in FAR_16 + (0,):
                    tile = lax.rem(z + d, ZS)

                    @pl.when(tile < TILES)
                    def _():
                        self.y_down(k, tile).start()

    def start_z(self):
        _, y, z, _ = self.pos
        for d in FAR_16 + (0,):
            tile = lax.rem(z + d, ZS)

            @pl.when(tile < TILES)
            def _():
                for k in range(1, YS):
                    self.y_down(k, tile).wait_recv()
                parts = [self.buf_y[k, tile] for k in range(YS - 1)]
                self.acc_y[tile] = self.acc_c[y, tile] + parts[0] + parts[1] + parts[2]
                if d:
                    self.z_down(d, tile).start()

    def start_z_back(self):
        _, y, z, c = self.pos

        @pl.when(z < TILES)
        def _():
            for d in range(1, ZS):
                self.z_down(d, 0).wait_recv()
            self.out[c, y, z] = self.acc_y[z] + sum(self.buf_z[d - 1] for d in range(1, ZS))
            for d in FAR_16:
                self.z_up(d, z).start()
            for d in FAR_4:
                self.y_up(d, self.out.at[c, y, z]).start()

    def start_y_back(self):
        _, y, z, c = self.pos
        for d in FAR_16[::-1]:
            source = lax.rem(z + ZS - d, ZS)

            @pl.when(source < TILES)
            def _():
                self.z_up(d, source).wait_recv()
                for e in FAR_4:
                    self.y_up(e, self.out.at[c, y, source]).start()

    def start_core_back(self):
        _, y, _, c = self.pos
        self.core_up(0, y).start()
        for d in (1, 3, 2):
            group = lax.rem(y + YS - d, YS)
            self.y_up(d, self.out.at[c, group]).wait_recv()
            self.core_up(d, group).start()

    def finish(self):
        for k in range(YS):
            group = lax.rem(self.pos[1] + YS - k, YS)
            piece = self.out.at[1 - self.pos[3], group]
            send(piece, piece, self.sc.at[1, k], self.rc.at[1, k], self.peers["c"]).wait_recv()

    def drain(self):
        _, y, z, c = self.pos
        for d in range(1, ZS):
            other = lax.rem(z + d, ZS)

            @pl.when(other < TILES)
            def _():
                self.z_down(d, other).wait_send()

        @pl.when(z < TILES)
        def _():
            for d in range(1, ZS):
                self.z_up(d, z).wait_send()

        for d in range(1, YS):
            self.y_up(d, self.out.at[c, y]).wait_send()
            self.y_down(d, None).wait_send()
        for k in range(YS):
            self.core_up(k, lax.rem(y + YS - k, YS)).wait_send()


def tile_place(tile):
    group, slot = divmod(tile, 12)
    return group // YS, group % YS, slot


def put_blocks(ref, moment, quad, result):
    first = lax.broadcasted_iota(jnp.int32, (E, 128), 1) < E
    for j in range(2):
        part = result[128 * j : 128 * j + 128, 128 * j : 128 * j + 128]
        block = jnp.where(first, part[0:E], part[E:128]).reshape(8, 8, 128)
        for half in range(2):
            c, y, slot = tile_place((moment * PAIRS + 2 * quad + j) * 8 + 4 * half)
            ref[c, y, pl.ds(slot, 4)] = block[4 * half : 4 * half + 4]


def row_place(moment, pair):
    row = moment * PAIRS + pair
    group = row // 2
    return group // YS, group % YS, row % 2


def put_row(ref, moment, pair, row):
    c, y, k = row_place(moment, pair)
    ref[c, y, TILES - 1, pl.ds(k, 1)] = row


def get_row(ref, moment, quad):
    rows = []
    for j in range(2):
        c, y, k = row_place(moment, 2 * quad + j)
        rows.append(ref[c, y, TILES - 1, pl.ds(k, 1)])
    return jnp.concatenate(rows, axis=1)


def get_blocks(ref, moment, quad, high_ref, low_ref):
    first = lax.broadcasted_iota(jnp.int32, (E, 128), 1) < E
    for j in range(2):
        halves = []
        for half in range(2):
            c, y, slot = tile_place((moment * PAIRS + 2 * quad + j) * 8 + 4 * half)
            halves.append(ref[c, y, pl.ds(slot, 4)].reshape(32, 128))
        block = jnp.concatenate(halves, axis=0)
        for k, kept in enumerate((jnp.where(first, block, 0.0), jnp.where(first, 0.0, block))):
            high, low = split(kept)
            here = pl.ds(128 * j + E * k, E), pl.ds(128 * j, 128)
            high_ref[moment, quad, here[0], here[1]] = high
            low_ref[moment, quad, here[0], here[1]] = low


class Scatter:
    def __init__(self, pos, peers, r, tag):
        self.pos, self.peers, self.r, self.tag = pos, peers, r, tag

    def ref(self, name):
        return self.r[name + self.tag]

    def put(self, name, result):
        xf, yf = self.ref(name + "x"), self.ref(name + "y")
        for y in range(YS):
            for x in range(XS):
                block = result[64 * y : 64 * y + 64, 128 * x : 128 * x + 128]
                xf[x, y] = block[0:32]
                yf[y, x] = block[32:64]

    def sems(self, phase, half, k):
        return self.ref("s" + phase).at[half, k], self.ref("r" + phase).at[half, k]

    def chunk(self, half, k):
        return lax.rem(self.pos[half] + k, 4)

    def core_copy(self, half, k):
        name, chunk = "xy"[half], self.chunk(half, k)
        return send(
            self.ref("send" + name).at[chunk], self.ref("got" + name).at[chunk], *self.sems("1", half, k), self.peers["c"]
        )

    def second_copy(self, half, d, k):
        name, part = "xy"[half], self.chunk(1 - half, k)
        return send(
            self.ref("own" + name).at[self.chunk(half, d), part], self.ref("b" + name).at[d - 1, part],
            self.ref("s2").at[half, d - 1, k], self.ref("r2").at[half, d - 1, k], self.peers[name][d - 1],
        )

    def third_copy(self, half, d):
        name, other = "xy"[half], "yx"[half]
        return send(
            self.ref("c" + name).at[self.chunk(1 - half, d)], self.ref("d" + name).at[d - 1],
            *self.sems("3", half, d - 1), self.peers[other][d - 1],
        )

    def last_copy(self, d):
        return send(
            self.ref("zs").at[lax.rem(self.pos[2] + d, ZS)], self.ref("zb").at[d - 1],
            self.ref("s4").at[d - 1], self.ref("r4").at[d - 1], self.peers["z"][d - 1],
        )

    def start_core(self):
        for k in FAR_4 + (0,):
            for half in range(2):
                self.core_copy(half, k).start()

    def start_second(self):
        for k in FAR_4 + (0,):
            for half in range(2):
                self.core_copy(half, k).wait()
                own, got = self.ref("own" + "xy"[half]), self.ref("got" + "xy"[half])
                chunk = self.chunk(half, k)
                own[chunk] = own[chunk] + got[chunk]
                if k:
                    for part in FAR_4 + (0,):
                        self.second_copy(half, k, part).start()

    def start_third(self):
        for k in FAR_4 + (0,):
            for half in range(2):
                name, part = "xy"[half], self.chunk(1 - half, k)
                for d in range(1, 4):
                    self.second_copy(half, d, k).wait()
                got, own = self.ref("b" + name), self.ref("own" + name)
                total = own[self.pos[half], part] + got[0, part] + got[1, part] + got[2, part]
                self.ref("c" + name)[part] = total
                if k:
                    self.third_copy(half, k).start()

    def start_last(self):
        zs = self.ref("zs")
        for half in range(2):
            for d in range(1, 4):
                self.third_copy(half, d).wait()
            got = self.ref("d" + "xy"[half])
            total = self.ref("c" + "xy"[half])[self.pos[1 - half]] + got[0] + got[1] + got[2]
            zs[8 * half : 8 * half + 8] = total.reshape(8, 4, 128)
        for d in FAR_16:
            self.last_copy(d).start()

    def finish(self, out, scale):
        for d in range(1, ZS):
            self.last_copy(d).wait()
        zb = self.ref("zb")
        out[...] = (self.ref("zs")[self.pos[2]] + sum(zb[d - 1] for d in range(1, ZS))) * scale


def reduce_scratch(tag):
    dma = pltpu.SemaphoreType.DMA
    return {
        "x" + tag: pltpu.VMEM((2, YS, TILES, 8, 128), F32),
        "out" + tag: pltpu.VMEM((2, YS, TILES, 8, 128), F32),
        "bufc" + tag: pltpu.VMEM((YS, TILES, 8, 128), F32),
        "accc" + tag: pltpu.VMEM((YS, TILES, 8, 128), F32),
        "bufy" + tag: pltpu.VMEM((YS - 1, TILES, 8, 128), F32),
        "accy" + tag: pltpu.VMEM((TILES, 8, 128), F32),
        "bufz" + tag: pltpu.VMEM((ZS - 1, 8, 128), F32),
        "sc" + tag: dma((2, YS)),
        "rc" + tag: dma((2, YS)),
        "sy" + tag: dma((2, YS - 1)),
        "ry" + tag: dma((2, YS - 1)),
        "ryd" + tag: dma((YS - 1, TILES)),
        "sz" + tag: dma((2, ZS - 1)),
        "rz" + tag: dma((2, ZS - 1)),
    }


def scatter_scratch(tag):
    dma = pltpu.SemaphoreType.DMA
    names = {}
    for axis in ("x", "y"):
        for kind in ("send", "got", "own"):
            names[kind + axis + tag] = pltpu.VMEM((4, 4, 32, 128), F32)
        names["b" + axis + tag] = pltpu.VMEM((3, 4, 32, 128), F32)
        names["c" + axis + tag] = pltpu.VMEM((4, 32, 128), F32)
        names["d" + axis + tag] = pltpu.VMEM((3, 32, 128), F32)
    names["zs" + tag] = pltpu.VMEM((ZS, 4, 128), F32)
    names["zb" + tag] = pltpu.VMEM((ZS - 1, 4, 128), F32)
    for k, shape in (("1", (2, 4)), ("2", (2, 3, 4)), ("3", (2, 3))):
        names["s" + k + tag] = dma(shape)
        names["r" + k + tag] = dma(shape)
    names["s4" + tag] = dma((ZS - 1,))
    names["r4" + tag] = dma((ZS - 1,))
    return names


def scratch():
    full = pltpu.VMEM((ROWS, D), F32)
    half = pltpu.VMEM((ROWS, D), BF16)
    names = {n: full for n in ("uq", "uk", "fq", "fk", "att", "rden", "gnum", "gden", "wtd", "gin")}
    names.update({n: half for n in ("fqh", "fql", "fkh", "fkl", "vh", "vl", "gnh", "gnl", "gq", "gk", "gv")})
    names["gh"] = pltpu.VMEM((ROWS, F), F32)
    names["turn"] = pltpu.VMEM((2, QUAD, ROWS), BF16)
    names["ones"] = pltpu.VMEM((QUAD, QUAD), BF16)
    names["ph"] = pltpu.VMEM((2, QUAD, QUAD), BF16)
    names["pl"] = pltpu.VMEM((2, QUAD, QUAD), BF16)
    for n in ("sh", "sl", "gsh", "gsl"):
        names[n] = pltpu.VMEM((T, 2, QUAD, QUAD), BF16)
    names.update(reduce_scratch("_1"))
    names.update(reduce_scratch("_2"))
    for tag in ("_q", "_k", "_v"):
        names.update(scatter_scratch(tag))
    for n, (shape, kind) in STAGED.items():
        names["in_" + n] = pltpu.VMEM(shape, kind)
    names["fetch"] = pltpu.SemaphoreType.DMA((len(STAGED),))
    return names


def kernel(
    scale, x_hbm, cot_hbm, wq_hbm, wk_hbm, wv_hbm, up_hbm, down_hbm, proj_hbm, live_ref,
    gin_ref, oq_ref, ok_ref, ov_ref, *rest,
):
    r = dict(zip(scratch().keys(), rest))
    sources = dict(
        x=x_hbm, cot=cot_hbm, wq=wq_hbm, wk=wk_hbm, wv=wv_hbm, up=up_hbm, down=down_hbm, proj=proj_hbm
    )
    fetches = {
        n: pltpu.make_async_copy(sources[n], r["in_" + n], r["fetch"].at[i]) for i, n in enumerate(STAGED)
    }
    start(fetches.values())

    def fetched(n):
        fetches[n].wait()
        return r["in_" + n]

    s = lax.axis_index("sensor")
    x, y, z, c = lax.axis_index("step"), s // (2 * ZS), lax.rem(s // 2, ZS), lax.rem(s, 2)
    pos = (x, y, z, c)
    peers = {
        "c": at(x, y, z, 1 - c),
        "y": [at(x, lax.rem(y + d, YS), z, c) for d in range(1, YS)],
        "x": [at(lax.rem(x + d, XS), y, z, c) for d in range(1, XS)],
        "z": [at(x, y, lax.rem(z + d, ZS), c) for d in range(1, ZS)],
    }
    everyone = [peers["c"]] + peers["y"] + peers["x"] + peers["z"]
    barrier = pltpu.get_barrier_semaphore()
    for target in everyone:
        pl.semaphore_signal(barrier, inc=1, device_id=target, device_id_type=MESH)

    row_id = lax.rem(lax.broadcasted_iota(jnp.int32, (ROWS, 1), 0), N)
    quads = [pl.ds(QUAD * q, QUAD) for q in range(2)]
    moments = [pl.ds(N * t, N) for t in range(T)]

    same = lax.broadcasted_iota(jnp.int32, (QUAD, QUAD), 0) // E == lax.broadcasted_iota(jnp.int32, (QUAD, QUAD), 1) // E
    r["ones"][...] = jnp.where(same, 1.0, 0.0).astype(BF16)
    ones = r["ones"]
    zero = jnp.zeros((E, E), F32)
    rows = fetched("x")[...].reshape(ROWS, D)
    r["uk"][...] = dot(rows, fetched("wk")[...]) * FACTOR
    proj_ref = fetched("proj")
    for q in range(2):
        lines = []
        for k in range(4):
            parts = [zero] * 4
            parts[k] = proj_ref[4 * q + k]
            lines.append(jnp.concatenate(parts, axis=1))
        r["ph"][q], r["pl"][q] = split(jnp.concatenate(lines, axis=0))

    def features(u_ref, q):
        u = u_ref[:, quads[q]]
        exponent = dot3(dot, split(u), (r["ph"][q], r["pl"][q])) - 0.5 * head_sum(u * u, ones[...])
        return jnp.exp(exponent) * (E ** -0.5)

    def feature_back(weighted, u, q):
        back = dot3(dot_nt, split(weighted), (r["ph"][q], r["pl"][q])) - u * head_sum(weighted, ones[...])
        return (back * FACTOR).astype(BF16)

    r["vh"][...], r["vl"][...] = split(dot(rows, fetched("wv")[...]))
    valid = row_id < live_ref[0]
    for q in range(2):
        fk = jnp.where(valid, features(r["uk"], q), 0.0)
        r["fk"][:, quads[q]] = fk
        r["fkh"][:, quads[q]], r["fkl"][:, quads[q]] = split(fk)

    def outer(a, b, t, q):
        (ah, al), (bh, bl) = a, b
        here = moments[t], quads[q]
        left = jnp.concatenate([ah[here], al[here], ah[here]], axis=0)
        right = jnp.concatenate([bh[here], bh[here], bl[here]], axis=0)
        return dot_tn(left, right)

    first, second = Reduce(pos, peers, r, "_1"), Reduce(pos, peers, r, "_2")
    for ref in (first.x, second.x):
        ref[:, :, TILES - 1] = jnp.zeros((2, YS, 8, 128), F32)
    for t in range(T):
        for q in range(2):
            put_blocks(first.x, t, q, outer((r["fkh"], r["fkl"]), (r["vh"], r["vl"]), t, q))
        total = jnp.sum(r["fk"][moments[t], :], axis=0, keepdims=True)
        for p in range(PAIRS):
            put_row(first.x, t, p, total[:, 128 * p : 128 * p + 128])

    pl.semaphore_wait(barrier, len(everyone))
    first.start_core()
    wq_ref = fetched("wq")
    r["uq"][...] = dot(rows, wq_ref[...]) * FACTOR
    first.start_y()
    for q in range(2):
        fq = features(r["uq"], q)
        r["fq"][:, quads[q]] = fq
        r["fqh"][:, quads[q]], r["fql"][:, quads[q]] = split(fq)
    first.start_z()
    masked = jnp.where(valid, fetched("cot")[...].reshape(ROWS, D), jnp.zeros((), BF16))
    r["gh"][...] = dot_nt(masked, fetched("down")[...])
    up_ref = fetched("up")
    for n in ("sh", "sl", "gsh", "gsl"):
        r[n][...] = jnp.zeros_like(r[n])
    first.start_z_back()
    line = lax.broadcasted_iota(jnp.int32, (QUAD, D), 0)
    column = lax.broadcasted_iota(jnp.int32, (QUAD, D), 1)
    for k in range(2):
        source = (line // 64) * 128 + lax.rem(line // 4, ZS) * 8 + 4 * k + lax.rem(line, 4)
        pick = jnp.where(source == column, 1.0, 0.0).astype(BF16)
        r["turn"][k] = dot_nt(pick, rows).astype(BF16)
    first.start_y_back()
    first.start_core_back()
    first.finish()

    for t in range(T):
        for q in range(2):
            here = moments[t], quads[q]
            get_blocks(first.out, t, q, r["sh"], r["sl"])
            numer = dot3(dot, (r["fqh"][here], r["fql"][here]), (r["sh"][t, q], r["sl"][t, q]))
            inverse = 1.0 / head_sum(r["fq"][here] * get_row(first.out, t, q), ones[...])
            r["rden"][here] = inverse
            r["att"][here] = numer * inverse
    att = r["att"][...]
    rms_inverse = 1.0 / jnp.sqrt(jnp.mean(att * att, axis=1, keepdims=True) + 1e-06)
    normed = att * rms_inverse
    pre = dot(normed.astype(BF16), up_ref[...])
    grad_pre = (r["gh"][...] * gelu_slope(pre)).astype(BF16)
    grad_normed = dot_nt(grad_pre, up_ref[...])
    mean = jnp.mean(grad_normed * normed, axis=1, keepdims=True)
    grad_att = (grad_normed - normed * mean) * rms_inverse
    for q in range(2):
        ga = grad_att[:, QUAD * q : QUAD * q + QUAD]
        inverse = r["rden"][:, quads[q]]
        gnum = ga * inverse
        r["gnum"][:, quads[q]] = gnum
        r["gnh"][:, quads[q]], r["gnl"][:, quads[q]] = split(gnum)
        r["gden"][:, quads[q]] = -head_sum(ga * r["att"][:, quads[q]], ones[...]) * inverse
    for t in range(T):
        for q in range(2):
            put_blocks(second.x, t, q, outer((r["fqh"], r["fql"]), (r["gnh"], r["gnl"]), t, q))
        total = jnp.sum(r["fq"][moments[t], :] * r["gden"][moments[t], :], axis=0, keepdims=True)
        for p in range(PAIRS):
            put_row(second.x, t, p, total[:, 128 * p : 128 * p + 128])

    second.start_core()
    for t in range(T):
        for q in range(2):
            here = moments[t], quads[q]
            gfq = dot3(dot_nt, (r["gnh"][here], r["gnl"][here]), (r["sh"][t, q], r["sl"][t, q]))
            gfq = gfq + r["gden"][here] * get_row(first.out, t, q)
            r["wtd"][here] = gfq * r["fq"][here]
    second.start_y()
    for q in range(2):
        r["gq"][:, quads[q]] = feature_back(r["wtd"][:, quads[q]], r["uq"][:, quads[q]], q)
    job_q, job_k, job_v = (Scatter(pos, peers, r, tag) for tag in ("_q", "_k", "_v"))
    job_q.put("send", dot(r["turn"][1 - c], r["gq"][...]))
    second.start_z()
    job_q.start_core()
    job_q.put("own", dot(r["turn"][c], r["gq"][...]))
    job_q.start_second()
    r["gin"][...] = dot_nt(r["gq"][...], wq_ref[...])
    second.start_z_back()
    second.start_y_back()
    job_q.start_third()
    second.start_core_back()
    second.finish()

    for t in range(T):
        for q in range(2):
            here = moments[t], quads[q]
            get_blocks(second.out, t, q, r["gsh"], r["gsl"])
            blocks = (r["gsh"][t, q], r["gsl"][t, q])
            r["gv"][here] = dot3(dot, (r["fkh"][here], r["fkl"][here]), blocks).astype(BF16)
    job_v.put("send", dot(r["turn"][1 - c], r["gv"][...]))
    job_v.start_core()
    job_q.start_last()
    for t in range(T):
        for q in range(2):
            here = moments[t], quads[q]
            blocks = (r["gsh"][t, q], r["gsl"][t, q])
            gfk = dot3(dot_nt, (r["vh"][here], r["vl"][here]), blocks) + get_row(second.out, t, q)
            r["wtd"][here] = gfk * r["fk"][here]
    for q in range(2):
        r["gk"][:, quads[q]] = feature_back(r["wtd"][:, quads[q]], r["uk"][:, quads[q]], q)
    job_k.put("send", dot(r["turn"][1 - c], r["gk"][...]))
    job_k.start_core()
    job_v.put("own", dot(r["turn"][c], r["gv"][...]))
    job_v.start_second()
    job_k.put("own", dot(r["turn"][c], r["gk"][...]))
    job_k.start_second()
    total = r["gin"][...] + dot_nt(r["gk"][...], r["in_wk"][...]) + dot_nt(r["gv"][...], r["in_wv"][...])
    gin_ref[...] = total.astype(BF16).reshape(T, N, D)
    job_v.start_third()
    job_k.start_third()
    job_v.start_last()
    job_k.start_last()
    job_q.finish(oq_ref, scale)
    job_v.finish(ov_ref, scale)
    job_k.finish(ok_ref, scale)
    first.drain()
    second.drain()


def hand_on(*refs):
    for source, target in zip(refs[:4], refs[4:]):
        target[...] = source[...]


def shards(inputs, cotangent, w_query, w_key, w_value, w_up, w_down, feature_proj, live_count):
    total_rows = T * XS * N * YS * ZS * 2
    piece = jax.ShapeDtypeStruct((4, 128), F32)
    shapes = (jax.ShapeDtypeStruct((T, N, D), BF16), piece, piece, piece)
    results = pl.pallas_call(
        functools.partial(kernel, 1.0 / math.sqrt(total_rows)),
        out_shape=shapes,
        in_specs=[ANY] * 8 + [SM],
        out_specs=(VM,) * 4,
        scratch_shapes=list(scratch().values()),
        compiler_params=pltpu.CompilerParams(collective_id=0, has_side_effects=True, vmem_limit_bytes=56 << 20),
    )(inputs, cotangent, w_query, w_key, w_value, w_up, w_down, feature_proj, live_count)
    return pl.pallas_call(
        hand_on,
        out_shape=shapes,
        in_specs=[VM] * 4,
        out_specs=(VM,) * 4,
    )(*results)


def solution(mesh):
    placed = (P("step", "sensor", None),) * 2 + (P(),) * 6 + (P("sensor"),)
    return jax.shard_map(
        shards,
        mesh=mesh,
        in_specs=placed,
        out_specs=(P("step", "sensor", None),) + (P("sensor", "step"),) * 3,
        check_vma=False,
    )
```

```python
import functools
import math

import jax
import jax.numpy as jnp
from jax import lax
from jax.experimental import pallas as pl
from jax.experimental.pallas import tpu as pltpu
from jax.sharding import PartitionSpec as P

MESH = pl.DeviceIdType.MESH
VM = pl.BlockSpec(memory_space=pltpu.VMEM)
SM = pl.BlockSpec(memory_space=pltpu.SMEM)
ANY = pl.BlockSpec(memory_space=pl.ANY)
F32, BF16 = jnp.float32, jnp.bfloat16
YS, ZS, XS = 4, 16, 4
T, N, D, F, H, E = 3, 64, 512, 256, 8, 64
ROWS = T * N
PAIRS = H // 2
TILES = 13
QUAD = 256
FACTOR = E ** (-0.25)
STAGED = {
    "x": ((T, N, D), BF16),
    "wk": ((D, D), BF16),
    "proj": ((H, E, E), F32),
    "wv": ((D, D), BF16),
    "wq": ((D, D), BF16),
    "cot": ((T, N, D), BF16),
    "down": ((F, D), BF16),
    "up": ((D, F), BF16),
}
FAR_4 = (2, 1, 3)
FAR_16 = (8, 7, 9, 6, 10, 5, 11, 4, 12, 3, 13, 2, 14, 1, 15)


def at(x, y, z, c):
    return ((y * ZS + z) * 2 + c, x)


def send(src, dst, ssem, rsem, target):
    return pltpu.make_async_remote_copy(
        src_ref=src, dst_ref=dst, send_sem=ssem, recv_sem=rsem, device_id=target, device_id_type=MESH
    )


def start(copies):
    for copy in copies:
        copy.start()


def wait(copies):
    for copy in copies:
        copy.wait()


def arrival(ref, landed, sent, peer):
    send(ref, ref, sent, landed, peer).wait_recv()


def departure(ref, sent, landed, peer):
    send(ref, ref, sent, landed, peer).wait_send()


def dot(a, b):
    return lax.dot_general(a, b, (((1,), (0,)), ((), ())), preferred_element_type=F32)


def dot_nt(a, b):
    return lax.dot_general(a, b, (((1,), (1,)), ((), ())), preferred_element_type=F32)


def dot_tn(a, b):
    return lax.dot_general(a, b, (((0,), (0,)), ((), ())), preferred_element_type=F32)


def split(value):
    high = value.astype(BF16)
    return high, (value - high.astype(F32)).astype(BF16)


def dot3(product, a, b):
    return product(a[0], b[0]) + product(a[1], b[0]) + product(a[0], b[1])


def head_sum(value, ones):
    high, low = split(value)
    return dot(high, ones) + dot(low, ones)


def gelu_slope(v):
    k = math.sqrt(2 / math.pi)
    th = jnp.tanh(k * (v + 0.044715 * v * v * v))
    return 0.5 * (1.0 + th) + 0.5 * v * (1.0 - th * th) * (k * (1.0 + 3 * 0.044715 * v * v))


class Reduce:
    def __init__(self, pos, peers, r, tag):
        self.pos, self.peers = pos, peers
        self.x, self.out = r["x" + tag], r["out" + tag]
        self.buf_c, self.acc_c = r["bufc" + tag], r["accc" + tag]
        self.buf_y, self.acc_y, self.buf_z = r["bufy" + tag], r["accy" + tag], r["bufz" + tag]
        self.sent, self.core_in, self.y_in = r["sent" + tag], r["corein" + tag], r["yin" + tag]
        self.z_in, self.z_out, self.y_out, self.core_out = r["zin" + tag], r["zout" + tag], r["yout" + tag], r["coreout" + tag]

    def core_down(self, k):
        chunk = lax.rem(self.pos[1] + k, YS)
        source = self.x.at[1 - self.pos[3], chunk]
        return send(source, self.buf_c.at[chunk], self.sent.at[0], self.core_in.at[k], self.peers["c"])

    def y_down(self, d, tile):
        chunk = lax.rem(self.pos[1] + d, YS)
        target = self.buf_y.at[tile, d - 1]
        return send(self.acc_c.at[chunk, tile], target, self.sent.at[1], self.y_in.at[tile], self.peers["y"][d - 1])

    def z_down(self, d, tile):
        return send(self.acc_y.at[tile], self.buf_z.at[d - 1], self.sent.at[2], self.z_in.at[0], self.peers["z"][d - 1])

    def z_up(self, d, tile):
        piece = self.out.at[self.pos[3], self.pos[1], tile]
        return send(piece, piece, self.sent.at[3], self.z_out.at[tile], self.peers["z"][d - 1])

    def y_up(self, d, piece):
        return send(piece, piece, self.sent.at[4], self.y_out.at[d - 1], self.peers["y"][d - 1])

    def core_up(self, group):
        piece = self.out.at[self.pos[3], group]
        return send(piece, piece, self.sent.at[5], self.core_out.at[0], self.peers["c"])

    def start_core(self):
        for k in FAR_4 + (0,):
            self.core_down(k).start()

    def start_y(self):
        _, y, z, c = self.pos
        for k in FAR_4 + (0,):
            self.core_down(k).wait_recv()
            chunk = lax.rem(y + k, YS)
            self.acc_c[chunk] = self.x[c, chunk] + self.buf_c[chunk]
            if k:
                for d in FAR_16 + (0,):
                    tile = lax.rem(z + d, ZS)

                    @pl.when(tile < TILES)
                    def _():
                        self.y_down(k, tile).start()

    def start_z(self):
        _, y, z, _ = self.pos
        for d in FAR_16 + (0,):
            tile = lax.rem(z + d, ZS)

            @pl.when(tile < TILES)
            def _():
                landed = self.buf_y.at[tile]
                arrival(landed, self.y_in.at[tile], self.sent.at[1], self.peers["c"])
                self.acc_y[tile] = self.acc_c[y, tile] + landed[0] + landed[1] + landed[2]
                if d:
                    self.z_down(d, tile).start()

    def start_z_back(self):
        _, y, z, c = self.pos

        @pl.when(z < TILES)
        def _():
            arrival(self.buf_z, self.z_in.at[0], self.sent.at[2], self.peers["c"])
            self.out[c, y, z] = self.acc_y[z] + sum(self.buf_z[d - 1] for d in range(1, ZS))
            for d in FAR_16:
                self.z_up(d, z).start()
            for d in FAR_4:
                self.y_up(d, self.out.at[c, y, z]).start()

    def start_y_back(self):
        _, y, z, c = self.pos
        for d in FAR_16[::-1]:
            source = lax.rem(z + ZS - d, ZS)

            @pl.when(source < TILES)
            def _():
                self.z_up(d, source).wait_recv()
                for e in FAR_4:
                    self.y_up(e, self.out.at[c, y, source]).start()

    def start_core_back(self):
        _, y, _, c = self.pos
        self.core_up(y).start()
        for d in (1, 3, 2):
            group = lax.rem(y + YS - d, YS)
            self.y_up(d, self.out.at[c, group]).wait_recv()
            self.core_up(group).start()

    def finish(self):
        arrival(self.out.at[1 - self.pos[3]], self.core_out.at[0], self.sent.at[5], self.peers["c"])

    def drain(self):
        z, peer = self.pos[2], self.peers["c"]
        departure(self.buf_c, self.sent.at[0], self.core_in.at[0], peer)
        departure(self.buf_y, self.sent.at[1], self.y_in.at[0], peer)
        departure(self.buf_y, self.sent.at[4], self.y_in.at[0], peer)
        departure(self.buf_c, self.sent.at[5], self.core_in.at[0], peer)

        @pl.when(z < TILES)
        def _():
            departure(self.acc_y.at[pl.ds(0, TILES - 1)], self.sent.at[2], self.z_in.at[0], peer)
            departure(self.buf_z, self.sent.at[3], self.z_in.at[0], peer)

        @pl.when(z >= TILES)
        def _():
            departure(self.acc_y, self.sent.at[2], self.z_in.at[0], peer)


def tile_place(tile):
    group, slot = divmod(tile, 12)
    return group // YS, group % YS, slot


def put_blocks(ref, moment, quad, result):
    first = lax.broadcasted_iota(jnp.int32, (E, 128), 1) < E
    for j in range(2):
        part = result[128 * j : 128 * j + 128, 128 * j : 128 * j + 128]
        block = jnp.where(first, part[0:E], part[E:128]).reshape(8, 8, 128)
        for half in range(2):
            c, y, slot = tile_place((moment * PAIRS + 2 * quad + j) * 8 + 4 * half)
            ref[c, y, pl.ds(slot, 4)] = block[4 * half : 4 * half + 4]


def row_place(moment, pair):
    row = moment * PAIRS + pair
    group = row // 2
    return group // YS, group % YS, row % 2


def put_row(ref, moment, pair, row):
    c, y, k = row_place(moment, pair)
    ref[c, y, TILES - 1, pl.ds(k, 1)] = row


def get_row(ref, moment, quad):
    rows = []
    for j in range(2):
        c, y, k = row_place(moment, 2 * quad + j)
        rows.append(ref[c, y, TILES - 1, pl.ds(k, 1)])
    return jnp.concatenate(rows, axis=1)


def get_blocks(ref, moment, quad, high_ref, low_ref):
    first = lax.broadcasted_iota(jnp.int32, (E, 128), 1) < E
    for j in range(2):
        halves = []
        for half in range(2):
            c, y, slot = tile_place((moment * PAIRS + 2 * quad + j) * 8 + 4 * half)
            halves.append(ref[c, y, pl.ds(slot, 4)].reshape(32, 128))
        block = jnp.concatenate(halves, axis=0)
        for k, kept in enumerate((jnp.where(first, block, 0.0), jnp.where(first, 0.0, block))):
            high, low = split(kept)
            here = pl.ds(128 * j + E * k, E), pl.ds(128 * j, 128)
            high_ref[moment, quad, here[0], here[1]] = high
            low_ref[moment, quad, here[0], here[1]] = low


class Scatter:
    def __init__(self, pos, peers, r, tag):
        self.pos, self.peers, self.r, self.tag = pos, peers, r, tag

    def ref(self, name):
        return self.r[name + self.tag]

    def put(self, name, result):
        xf, yf = self.ref(name + "x"), self.ref(name + "y")
        for y in range(YS):
            for x in range(XS):
                block = result[64 * y : 64 * y + 64, 128 * x : 128 * x + 128]
                xf[x, y] = block[0:32]
                yf[y, x] = block[32:64]

    def chunk(self, half, k):
        return lax.rem(self.pos[half] + k, 4)

    def sent(self, phase, half):
        return self.ref("sent").at[2 * phase + half]

    def core_copy(self, half, k):
        name, chunk = "xy"[half], self.chunk(half, k)
        return send(
            self.ref("send" + name).at[chunk], self.ref("got" + name).at[chunk], self.sent(0, half),
            self.ref("in1").at[half, k], self.peers["c"],
        )

    def second_copy(self, half, d, k):
        name, part = "xy"[half], self.chunk(1 - half, k)
        return send(
            self.ref("own" + name).at[self.chunk(half, d), part], self.ref("b" + name).at[part, d - 1],
            self.sent(1, half), self.ref("in2").at[half, k], self.peers[name][d - 1],
        )

    def third_copy(self, half, d):
        name, other = "xy"[half], "yx"[half]
        return send(
            self.ref("c" + name).at[self.chunk(1 - half, d)], self.ref("d" + name).at[d - 1],
            self.sent(2, half), self.ref("in3").at[half], self.peers[other][d - 1],
        )

    def last_copy(self, d):
        return send(
            self.ref("zs").at[lax.rem(self.pos[2] + d, ZS)], self.ref("zb").at[d - 1],
            self.sent(3, 0), self.ref("in3").at[2], self.peers["z"][d - 1],
        )

    def start_core(self):
        for k in FAR_4 + (0,):
            for half in range(2):
                self.core_copy(half, k).start()

    def start_second(self):
        for k in FAR_4 + (0,):
            for half in range(2):
                self.core_copy(half, k).wait_recv()
                own, got = self.ref("own" + "xy"[half]), self.ref("got" + "xy"[half])
                chunk = self.chunk(half, k)
                own[chunk] = own[chunk] + got[chunk]
                if k:
                    for part in FAR_4 + (0,):
                        self.second_copy(half, k, part).start()

    def start_third(self):
        for k in FAR_4 + (0,):
            for half in range(2):
                name, part = "xy"[half], self.chunk(1 - half, k)
                landed, own = self.ref("b" + name).at[part], self.ref("own" + name)
                arrival(landed, self.ref("in2").at[half, k], self.sent(1, half), self.peers["c"])
                self.ref("c" + name)[part] = own[self.pos[half], part] + landed[0] + landed[1] + landed[2]
                if k:
                    self.third_copy(half, k).start()

    def start_last(self):
        zs = self.ref("zs")
        for half in range(2):
            landed = self.ref("d" + "xy"[half])
            arrival(landed, self.ref("in3").at[half], self.sent(2, half), self.peers["c"])
            total = self.ref("c" + "xy"[half])[self.pos[1 - half]] + landed[0] + landed[1] + landed[2]
            zs[8 * half : 8 * half + 8] = total.reshape(8, 4, 128)
        for d in FAR_16:
            self.last_copy(d).start()

    def finish(self, out, scale):
        zb = self.ref("zb")
        arrival(zb, self.ref("in3").at[2], self.sent(3, 0), self.peers["c"])
        out[...] = (self.ref("zs")[self.pos[2]] + sum(zb[d - 1] for d in range(1, ZS))) * scale

    def drain(self):
        spare = self.ref("in3").at[0]
        for half, name in enumerate("xy"):
            departure(self.ref("send" + name), self.sent(0, half), spare, self.peers["c"])
            departure(self.ref("b" + name), self.sent(1, half), spare, self.peers["c"])
            departure(self.ref("d" + name), self.sent(2, half), spare, self.peers["c"])
        departure(self.ref("zb"), self.sent(3, 0), spare, self.peers["c"])


def reduce_scratch(tag):
    dma = pltpu.SemaphoreType.DMA
    return {
        "x" + tag: pltpu.VMEM((2, YS, TILES, 8, 128), F32),
        "out" + tag: pltpu.VMEM((2, YS, TILES, 8, 128), F32),
        "bufc" + tag: pltpu.VMEM((YS, TILES, 8, 128), F32),
        "accc" + tag: pltpu.VMEM((YS, TILES, 8, 128), F32),
        "bufy" + tag: pltpu.VMEM((TILES, YS - 1, 8, 128), F32),
        "accy" + tag: pltpu.VMEM((TILES, 8, 128), F32),
        "bufz" + tag: pltpu.VMEM((ZS - 1, 8, 128), F32),
        "sent" + tag: dma((6,)),
        "corein" + tag: dma((YS,)),
        "yin" + tag: dma((TILES,)),
        "zin" + tag: dma((1,)),
        "zout" + tag: dma((TILES,)),
        "yout" + tag: dma((YS - 1,)),
        "coreout" + tag: dma((1,)),
    }


def scatter_scratch(tag):
    dma = pltpu.SemaphoreType.DMA
    names = {}
    for axis in ("x", "y"):
        for kind in ("send", "got", "own"):
            names[kind + axis + tag] = pltpu.VMEM((4, 4, 32, 128), F32)
        names["b" + axis + tag] = pltpu.VMEM((4, 3, 32, 128), F32)
        names["c" + axis + tag] = pltpu.VMEM((4, 32, 128), F32)
        names["d" + axis + tag] = pltpu.VMEM((3, 32, 128), F32)
    names["zs" + tag] = pltpu.VMEM((ZS, 4, 128), F32)
    names["zb" + tag] = pltpu.VMEM((ZS - 1, 4, 128), F32)
    names["sent" + tag] = dma((7,))
    names["in1" + tag] = dma((2, 4))
    names["in2" + tag] = dma((2, 4))
    names["in3" + tag] = dma((3,))
    return names


def scratch():
    full = pltpu.VMEM((ROWS, D), F32)
    half = pltpu.VMEM((ROWS, D), BF16)
    names = {n: full for n in ("uq", "uk", "fq", "fk", "att", "rden", "gnum", "gden", "wtd", "gin")}
    names.update({n: half for n in ("fqh", "fql", "fkh", "fkl", "vh", "vl", "gnh", "gnl", "gq", "gk", "gv")})
    names["gh"] = pltpu.VMEM((ROWS, F), F32)
    names["turn"] = pltpu.VMEM((2, QUAD, ROWS), BF16)
    names["ones"] = pltpu.VMEM((QUAD, QUAD), BF16)
    names["ph"] = pltpu.VMEM((2, QUAD, QUAD), BF16)
    names["pl"] = pltpu.VMEM((2, QUAD, QUAD), BF16)
    for n in ("sh", "sl", "gsh", "gsl"):
        names[n] = pltpu.VMEM((T, 2, QUAD, QUAD), BF16)
    names.update(reduce_scratch("_1"))
    names.update(reduce_scratch("_2"))
    for tag in ("_q", "_k", "_v"):
        names.update(scatter_scratch(tag))
    for n, (shape, kind) in STAGED.items():
        names["in_" + n] = pltpu.VMEM(shape, kind)
    names["fetch"] = pltpu.SemaphoreType.DMA((len(STAGED),))
    return names


def kernel(
    scale, x_hbm, cot_hbm, wq_hbm, wk_hbm, wv_hbm, up_hbm, down_hbm, proj_hbm, live_ref,
    gin_ref, oq_ref, ok_ref, ov_ref, *rest,
):
    r = dict(zip(scratch().keys(), rest))
    sources = dict(
        x=x_hbm, cot=cot_hbm, wq=wq_hbm, wk=wk_hbm, wv=wv_hbm, up=up_hbm, down=down_hbm, proj=proj_hbm
    )
    fetches = {
        n: pltpu.make_async_copy(sources[n], r["in_" + n], r["fetch"].at[i]) for i, n in enumerate(STAGED)
    }
    start(fetches.values())

    def fetched(n):
        fetches[n].wait()
        return r["in_" + n]

    s = lax.axis_index("sensor")
    x, y, z, c = lax.axis_index("step"), s // (2 * ZS), lax.rem(s // 2, ZS), lax.rem(s, 2)
    pos = (x, y, z, c)
    peers = {
        "c": at(x, y, z, 1 - c),
        "y": [at(x, lax.rem(y + d, YS), z, c) for d in range(1, YS)],
        "x": [at(lax.rem(x + d, XS), y, z, c) for d in range(1, XS)],
        "z": [at(x, y, lax.rem(z + d, ZS), c) for d in range(1, ZS)],
    }
    everyone = [peers["c"]] + peers["y"] + peers["x"] + peers["z"]
    barrier = pltpu.get_barrier_semaphore()
    for target in everyone:
        pl.semaphore_signal(barrier, inc=1, device_id=target, device_id_type=MESH)

    row_id = lax.rem(lax.broadcasted_iota(jnp.int32, (ROWS, 1), 0), N)
    quads = [pl.ds(QUAD * q, QUAD) for q in range(2)]
    moments = [pl.ds(N * t, N) for t in range(T)]

    same = lax.broadcasted_iota(jnp.int32, (QUAD, QUAD), 0) // E == lax.broadcasted_iota(jnp.int32, (QUAD, QUAD), 1) // E
    r["ones"][...] = jnp.where(same, 1.0, 0.0).astype(BF16)
    ones = r["ones"]
    zero = jnp.zeros((E, E), F32)
    rows = fetched("x")[...].reshape(ROWS, D)
    r["uk"][...] = dot(rows, fetched("wk")[...]) * FACTOR
    proj_ref = fetched("proj")
    for q in range(2):
        lines = []
        for k in range(4):
            parts = [zero] * 4
            parts[k] = proj_ref[4 * q + k]
            lines.append(jnp.concatenate(parts, axis=1))
        r["ph"][q], r["pl"][q] = split(jnp.concatenate(lines, axis=0))

    def features(u_ref, q):
        u = u_ref[:, quads[q]]
        exponent = dot3(dot, split(u), (r["ph"][q], r["pl"][q])) - 0.5 * head_sum(u * u, ones[...])
        return jnp.exp(exponent) * (E ** -0.5)

    def feature_back(weighted, u, q):
        back = dot3(dot_nt, split(weighted), (r["ph"][q], r["pl"][q])) - u * head_sum(weighted, ones[...])
        return (back * FACTOR).astype(BF16)

    r["vh"][...], r["vl"][...] = split(dot(rows, fetched("wv")[...]))
    valid = row_id < live_ref[0]
    for q in range(2):
        fk = jnp.where(valid, features(r["uk"], q), 0.0)
        r["fk"][:, quads[q]] = fk
        r["fkh"][:, quads[q]], r["fkl"][:, quads[q]] = split(fk)

    def outer(a, b, t, q):
        (ah, al), (bh, bl) = a, b
        here = moments[t], quads[q]
        left = jnp.concatenate([ah[here], al[here], ah[here]], axis=0)
        right = jnp.concatenate([bh[here], bh[here], bl[here]], axis=0)
        return dot_tn(left, right)

    first, second = Reduce(pos, peers, r, "_1"), Reduce(pos, peers, r, "_2")
    for ref in (first.x, second.x):
        ref[:, :, TILES - 1] = jnp.zeros((2, YS, 8, 128), F32)
    for t in range(T):
        for q in range(2):
            put_blocks(first.x, t, q, outer((r["fkh"], r["fkl"]), (r["vh"], r["vl"]), t, q))
        total = jnp.sum(r["fk"][moments[t], :], axis=0, keepdims=True)
        for p in range(PAIRS):
            put_row(first.x, t, p, total[:, 128 * p : 128 * p + 128])

    pl.semaphore_wait(barrier, len(everyone))
    first.start_core()
    wq_ref = fetched("wq")
    r["uq"][...] = dot(rows, wq_ref[...]) * FACTOR
    first.start_y()
    for q in range(2):
        fq = features(r["uq"], q)
        r["fq"][:, quads[q]] = fq
        r["fqh"][:, quads[q]], r["fql"][:, quads[q]] = split(fq)
    first.start_z()
    masked = jnp.where(valid, fetched("cot")[...].reshape(ROWS, D), jnp.zeros((), BF16))
    r["gh"][...] = dot_nt(masked, fetched("down")[...])
    up_ref = fetched("up")
    for n in ("sh", "sl", "gsh", "gsl"):
        r[n][...] = jnp.zeros_like(r[n])
    first.start_z_back()
    line = lax.broadcasted_iota(jnp.int32, (QUAD, D), 0)
    column = lax.broadcasted_iota(jnp.int32, (QUAD, D), 1)
    for k in range(2):
        source = (line // 64) * 128 + lax.rem(line // 4, ZS) * 8 + 4 * k + lax.rem(line, 4)
        pick = jnp.where(source == column, 1.0, 0.0).astype(BF16)
        r["turn"][k] = dot_nt(pick, rows).astype(BF16)
    first.start_y_back()
    first.start_core_back()
    first.finish()

    for t in range(T):
        for q in range(2):
            here = moments[t], quads[q]
            get_blocks(first.out, t, q, r["sh"], r["sl"])
            numer = dot3(dot, (r["fqh"][here], r["fql"][here]), (r["sh"][t, q], r["sl"][t, q]))
            inverse = 1.0 / head_sum(r["fq"][here] * get_row(first.out, t, q), ones[...])
            r["rden"][here] = inverse
            r["att"][here] = numer * inverse
    att = r["att"][...]
    rms_inverse = 1.0 / jnp.sqrt(jnp.mean(att * att, axis=1, keepdims=True) + 1e-06)
    normed = att * rms_inverse
    pre = dot(normed.astype(BF16), up_ref[...])
    grad_pre = (r["gh"][...] * gelu_slope(pre)).astype(BF16)
    grad_normed = dot_nt(grad_pre, up_ref[...])
    mean = jnp.mean(grad_normed * normed, axis=1, keepdims=True)
    grad_att = (grad_normed - normed * mean) * rms_inverse
    for q in range(2):
        ga = grad_att[:, QUAD * q : QUAD * q + QUAD]
        inverse = r["rden"][:, quads[q]]
        gnum = ga * inverse
        r["gnum"][:, quads[q]] = gnum
        r["gnh"][:, quads[q]], r["gnl"][:, quads[q]] = split(gnum)
        r["gden"][:, quads[q]] = -head_sum(ga * r["att"][:, quads[q]], ones[...]) * inverse
    for t in range(T):
        for q in range(2):
            put_blocks(second.x, t, q, outer((r["fqh"], r["fql"]), (r["gnh"], r["gnl"]), t, q))
        total = jnp.sum(r["fq"][moments[t], :] * r["gden"][moments[t], :], axis=0, keepdims=True)
        for p in range(PAIRS):
            put_row(second.x, t, p, total[:, 128 * p : 128 * p + 128])

    second.start_core()
    for t in range(T):
        for q in range(2):
            here = moments[t], quads[q]
            gfq = dot3(dot_nt, (r["gnh"][here], r["gnl"][here]), (r["sh"][t, q], r["sl"][t, q]))
            gfq = gfq + r["gden"][here] * get_row(first.out, t, q)
            r["wtd"][here] = gfq * r["fq"][here]
    second.start_y()
    for q in range(2):
        r["gq"][:, quads[q]] = feature_back(r["wtd"][:, quads[q]], r["uq"][:, quads[q]], q)
    job_q, job_k, job_v = (Scatter(pos, peers, r, tag) for tag in ("_q", "_k", "_v"))
    job_q.put("send", dot(r["turn"][1 - c], r["gq"][...]))
    second.start_z()
    job_q.start_core()
    job_q.put("own", dot(r["turn"][c], r["gq"][...]))
    job_q.start_second()
    r["gin"][...] = dot_nt(r["gq"][...], wq_ref[...])
    second.start_z_back()
    second.start_y_back()
    job_q.start_third()
    second.start_core_back()
    second.finish()

    for t in range(T):
        for q in range(2):
            here = moments[t], quads[q]
            get_blocks(second.out, t, q, r["gsh"], r["gsl"])
            blocks = (r["gsh"][t, q], r["gsl"][t, q])
            r["gv"][here] = dot3(dot, (r["fkh"][here], r["fkl"][here]), blocks).astype(BF16)
    job_v.put("send", dot(r["turn"][1 - c], r["gv"][...]))
    job_v.start_core()
    job_q.start_last()
    for t in range(T):
        for q in range(2):
            here = moments[t], quads[q]
            blocks = (r["gsh"][t, q], r["gsl"][t, q])
            gfk = dot3(dot_nt, (r["vh"][here], r["vl"][here]), blocks) + get_row(second.out, t, q)
            r["wtd"][here] = gfk * r["fk"][here]
    for q in range(2):
        r["gk"][:, quads[q]] = feature_back(r["wtd"][:, quads[q]], r["uk"][:, quads[q]], q)
    job_k.put("send", dot(r["turn"][1 - c], r["gk"][...]))
    job_k.start_core()
    job_v.put("own", dot(r["turn"][c], r["gv"][...]))
    job_v.start_second()
    job_k.put("own", dot(r["turn"][c], r["gk"][...]))
    job_k.start_second()
    total = r["gin"][...] + dot_nt(r["gk"][...], r["in_wk"][...]) + dot_nt(r["gv"][...], r["in_wv"][...])
    gin_ref[...] = total.astype(BF16).reshape(T, N, D)
    job_v.start_third()
    job_k.start_third()
    job_v.start_last()
    job_k.start_last()
    job_q.finish(oq_ref, scale)
    job_v.finish(ov_ref, scale)
    job_k.finish(ok_ref, scale)
    for job in (first, second, job_q, job_k, job_v):
        job.drain()


def hand_on(*refs):
    for source, target in zip(refs[:4], refs[4:]):
        target[...] = source[...]


def shards(inputs, cotangent, w_query, w_key, w_value, w_up, w_down, feature_proj, live_count):
    total_rows = T * XS * N * YS * ZS * 2
    piece = jax.ShapeDtypeStruct((4, 128), F32)
    shapes = (jax.ShapeDtypeStruct((T, N, D), BF16), piece, piece, piece)
    results = pl.pallas_call(
        functools.partial(kernel, 1.0 / math.sqrt(total_rows)),
        out_shape=shapes,
        in_specs=[ANY] * 8 + [SM],
        out_specs=(VM,) * 4,
        scratch_shapes=list(scratch().values()),
        compiler_params=pltpu.CompilerParams(collective_id=0, has_side_effects=True, vmem_limit_bytes=56 << 20),
    )(inputs, cotangent, w_query, w_key, w_value, w_up, w_down, feature_proj, live_count)
    return pl.pallas_call(
        hand_on,
        out_shape=shapes,
        in_specs=[VM] * 4,
        out_specs=(VM,) * 4,
    )(*results)


def solution(mesh):
    placed = (P("step", "sensor", None),) * 2 + (P(),) * 6 + (P("sensor"),)
    return jax.shard_map(
        shards,
        mesh=mesh,
        in_specs=placed,
        out_specs=(P("step", "sensor", None),) + (P("sensor", "step"),) * 3,
        check_vma=False,
    )
```

```python
import functools
import math

import jax
import jax.numpy as jnp
from jax import lax
from jax.experimental import pallas as pl
from jax.experimental.pallas import tpu as pltpu
from jax.sharding import PartitionSpec as P

MESH = pl.DeviceIdType.MESH
VM = pl.BlockSpec(memory_space=pltpu.VMEM)
SM = pl.BlockSpec(memory_space=pltpu.SMEM)
ANY = pl.BlockSpec(memory_space=pl.ANY)
F32, BF16 = jnp.float32, jnp.bfloat16
YS, ZS, XS = 4, 16, 4
T, N, D, F, H, E = 3, 64, 512, 256, 8, 64
ROWS = T * N
PAIRS = H // 2
TILES = 13
QUAD = 256
FACTOR = E ** (-0.25)
STAGED = {
    "x": ((T, N, D), BF16),
    "wk": ((D, D), BF16),
    "proj": ((H, E, E), F32),
    "wv": ((D, D), BF16),
    "wq": ((D, D), BF16),
    "cot": ((T, N, D), BF16),
    "down": ((F, D), BF16),
    "up": ((D, F), BF16),
}
FAR_4 = (2, 1, 3)
FAR_16 = (8, 7, 9, 6, 10, 5, 11, 4, 12, 3, 13, 2, 14, 1, 15)


def at(x, y, z, c):
    return ((y * ZS + z) * 2 + c, x)


def send(src, dst, ssem, rsem, target):
    return pltpu.make_async_remote_copy(
        src_ref=src, dst_ref=dst, send_sem=ssem, recv_sem=rsem, device_id=target, device_id_type=MESH
    )


def start(copies):
    for copy in copies:
        copy.start()


def wait(copies):
    for copy in copies:
        copy.wait()


def arrival(ref, landed, sent, peer):
    send(ref, ref, sent, landed, peer).wait_recv()


def departure(ref, sent, landed, peer):
    send(ref, ref, sent, landed, peer).wait_send()


def dot(a, b):
    return lax.dot_general(a, b, (((1,), (0,)), ((), ())), preferred_element_type=F32)


def dot_nt(a, b):
    return lax.dot_general(a, b, (((1,), (1,)), ((), ())), preferred_element_type=F32)


def dot_tn(a, b):
    return lax.dot_general(a, b, (((0,), (0,)), ((), ())), preferred_element_type=F32)


def split(value):
    high = value.astype(BF16)
    return high, (value - high.astype(F32)).astype(BF16)


def dot3(product, a, b):
    return product(a[0], b[0]) + product(a[1], b[0]) + product(a[0], b[1])


def head_sum(value, ones):
    high, low = split(value)
    return dot(high, ones) + dot(low, ones)


def gelu_slope(v):
    k = math.sqrt(2 / math.pi)
    th = jnp.tanh(k * (v + 0.044715 * v * v * v))
    return 0.5 * (1.0 + th) + 0.5 * v * (1.0 - th * th) * (k * (1.0 + 3 * 0.044715 * v * v))


class Reduce:
    def __init__(self, pos, peers, r, tag):
        self.pos, self.peers = pos, peers
        self.x, self.out = r["x" + tag], r["out" + tag]
        self.buf_c, self.acc_c = r["bufc" + tag], r["accc" + tag]
        self.buf_y, self.acc_y, self.buf_z = r["bufy" + tag], r["accy" + tag], r["bufz" + tag]
        self.sent, self.core_in, self.y_in = r["sent" + tag], r["corein" + tag], r["yin" + tag]
        self.z_in, self.z_out, self.y_out, self.core_out = r["zin" + tag], r["zout" + tag], r["yout" + tag], r["coreout" + tag]
        self.cross = r["cross" + tag]

    def core_down(self, k):
        chunk = lax.rem(self.pos[1] + k, YS)
        source = self.x.at[1 - self.pos[3], chunk]
        return send(source, self.buf_c.at[chunk], self.sent.at[0], self.core_in.at[k], self.peers["c"])

    def y_down(self, d, tile):
        chunk = lax.rem(self.pos[1] + d, YS)
        target = self.buf_y.at[tile, d - 1]
        return send(self.acc_c.at[chunk, tile], target, self.sent.at[1], self.y_in.at[tile], self.peers["y"][d - 1])

    def z_down(self, d, tile):
        return send(self.acc_y.at[tile], self.buf_z.at[d - 1], self.sent.at[2], self.z_in.at[0], self.peers["z"][d - 1])

    def z_up(self, d, tile):
        piece = self.out.at[self.pos[3], self.pos[1], tile]
        return send(piece, piece, self.sent.at[3], self.z_out.at[tile], self.peers["z"][d - 1])

    def y_up(self, d, piece):
        return send(piece, piece, self.sent.at[4], self.y_out.at[d - 1], self.peers["y"][d - 1])

    def cross_up(self, piece):
        return send(piece, piece, self.sent.at[6], self.cross.at[0], self.peers["far"])

    def core_up(self, group):
        piece = self.out.at[self.pos[3], group]
        return send(piece, piece, self.sent.at[5], self.core_out.at[0], self.peers["c"])

    def start_core(self):
        for k in FAR_4 + (0,):
            self.core_down(k).start()

    def start_y(self):
        _, y, z, c = self.pos
        for k in FAR_4 + (0,):
            self.core_down(k).wait_recv()
            chunk = lax.rem(y + k, YS)
            self.acc_c[chunk] = self.x[c, chunk] + self.buf_c[chunk]
            if k:
                for d in FAR_16 + (0,):
                    tile = lax.rem(z + d, ZS)

                    @pl.when(tile < TILES)
                    def _():
                        self.y_down(k, tile).start()

    def start_z(self):
        _, y, z, _ = self.pos
        for d in FAR_16 + (0,):
            tile = lax.rem(z + d, ZS)

            @pl.when(tile < TILES)
            def _():
                landed = self.buf_y.at[tile]
                arrival(landed, self.y_in.at[tile], self.sent.at[1], self.peers["c"])
                self.acc_y[tile] = self.acc_c[y, tile] + landed[0] + landed[1] + landed[2]
                if d:
                    self.z_down(d, tile).start()

    def start_z_back(self):
        _, y, z, c = self.pos

        @pl.when(z < TILES)
        def _():
            arrival(self.buf_z, self.z_in.at[0], self.sent.at[2], self.peers["c"])
            self.out[c, y, z] = self.acc_y[z] + sum(self.buf_z[d - 1] for d in range(1, ZS))
            for d in FAR_16:
                self.z_up(d, z).start()
            self.cross_up(self.out.at[c, y, z]).start()
            for d in FAR_4:
                self.y_up(d, self.out.at[c, y, z]).start()

    def start_y_back(self):
        _, y, z, c = self.pos
        for d in FAR_16[::-1]:
            source = lax.rem(z + ZS - d, ZS)

            @pl.when(source < TILES)
            def _():
                self.z_up(d, source).wait_recv()
                self.cross_up(self.out.at[c, y, source]).start()
                for e in FAR_4:
                    self.y_up(e, self.out.at[c, y, source]).start()

    def start_core_back(self):
        _, y, _, c = self.pos
        self.core_up(y).start()
        for d in (1, 3):
            group = lax.rem(y + YS - d, YS)
            self.y_up(d, self.out.at[c, group]).wait_recv()
            self.core_up(group).start()

    def finish(self):
        _, y, _, c = self.pos
        far = lax.rem(y + 2, YS)
        self.y_up(2, self.out.at[c, far]).wait_recv()
        arrival(self.out.at[1 - c, far], self.cross.at[0], self.sent.at[6], self.peers["far"])
        arrival(self.buf_y, self.core_out.at[0], self.sent.at[5], self.peers["c"])

    def drain(self):
        z, peer = self.pos[2], self.peers["c"]
        departure(self.buf_c, self.sent.at[0], self.core_in.at[0], peer)
        departure(self.buf_y, self.sent.at[1], self.y_in.at[0], peer)
        departure(self.buf_y, self.sent.at[4], self.y_in.at[0], peer)
        departure(self.buf_y, self.sent.at[5], self.core_in.at[0], peer)
        departure(self.acc_y, self.sent.at[6], self.core_in.at[0], peer)

        @pl.when(z < TILES)
        def _():
            departure(self.acc_y.at[pl.ds(0, TILES - 1)], self.sent.at[2], self.z_in.at[0], peer)
            departure(self.buf_z, self.sent.at[3], self.z_in.at[0], peer)

        @pl.when(z >= TILES)
        def _():
            departure(self.acc_y, self.sent.at[2], self.z_in.at[0], peer)


def tile_place(tile):
    group, slot = divmod(tile, 12)
    return group // YS, group % YS, slot


def put_blocks(ref, moment, quad, result):
    first = lax.broadcasted_iota(jnp.int32, (E, 128), 1) < E
    for j in range(2):
        part = result[128 * j : 128 * j + 128, 128 * j : 128 * j + 128]
        block = jnp.where(first, part[0:E], part[E:128]).reshape(8, 8, 128)
        for half in range(2):
            c, y, slot = tile_place((moment * PAIRS + 2 * quad + j) * 8 + 4 * half)
            ref[c, y, pl.ds(slot, 4)] = block[4 * half : 4 * half + 4]


def row_place(moment, pair):
    row = moment * PAIRS + pair
    group = row // 2
    return group // YS, group % YS, row % 2


def put_row(ref, moment, pair, row):
    c, y, k = row_place(moment, pair)
    ref[c, y, TILES - 1, pl.ds(k, 1)] = row


def get_row(ref, moment, quad):
    rows = []
    for j in range(2):
        c, y, k = row_place(moment, 2 * quad + j)
        rows.append(ref[c, y, TILES - 1, pl.ds(k, 1)])
    return jnp.concatenate(rows, axis=1)


def get_blocks(ref, moment, quad, high_ref, low_ref):
    first = lax.broadcasted_iota(jnp.int32, (E, 128), 1) < E
    for j in range(2):
        halves = []
        for half in range(2):
            c, y, slot = tile_place((moment * PAIRS + 2 * quad + j) * 8 + 4 * half)
            halves.append(ref[c, y, pl.ds(slot, 4)].reshape(32, 128))
        block = jnp.concatenate(halves, axis=0)
        for k, kept in enumerate((jnp.where(first, block, 0.0), jnp.where(first, 0.0, block))):
            high, low = split(kept)
            here = pl.ds(128 * j + E * k, E), pl.ds(128 * j, 128)
            high_ref[moment, quad, here[0], here[1]] = high
            low_ref[moment, quad, here[0], here[1]] = low


class Scatter:
    def __init__(self, pos, peers, r, tag):
        self.pos, self.peers, self.r, self.tag = pos, peers, r, tag

    def ref(self, name):
        return self.r[name + self.tag]

    def put(self, name, result):
        xf, yf = self.ref(name + "x"), self.ref(name + "y")
        for y in range(YS):
            for x in range(XS):
                block = result[64 * y : 64 * y + 64, 128 * x : 128 * x + 128]
                xf[x, y] = block[0:32]
                yf[y, x] = block[32:64]

    def chunk(self, half, k):
        return lax.rem(self.pos[half] + k, 4)

    def sent(self, phase, half):
        return self.ref("sent").at[2 * phase + half]

    def core_copy(self, half, k):
        name, chunk = "xy"[half], self.chunk(half, k)
        return send(
            self.ref("send" + name).at[chunk], self.ref("got" + name).at[chunk], self.sent(0, half),
            self.ref("in1").at[k], self.peers["c"],
        )

    def second_copy(self, half, d, k):
        name, part = "xy"[half], self.chunk(1 - half, k)
        return send(
            self.ref("own" + name).at[self.chunk(half, d), part], self.ref("b" + name).at[part, d - 1],
            self.sent(1, half), self.ref("in2").at[k], self.peers[name][d - 1],
        )

    def third_copy(self, half, d):
        name, other = "xy"[half], "yx"[half]
        return send(
            self.ref("c" + name).at[self.chunk(1 - half, d)], self.ref("d" + name).at[d - 1],
            self.sent(2, half), self.ref("in3").at[half], self.peers[other][d - 1],
        )

    def last_copy(self, d):
        return send(
            self.ref("zs").at[lax.rem(self.pos[2] + d, ZS)], self.ref("zb").at[d - 1],
            self.sent(3, 0), self.ref("in3").at[2], self.peers["z"][d - 1],
        )

    def start_core(self):
        for k in FAR_4 + (0,):
            for half in range(2):
                self.core_copy(half, k).start()

    def start_second(self):
        for k in FAR_4 + (0,):
            arrival(self.ref("gotx").at[pl.ds(0, 2)], self.ref("in1").at[k], self.sent(0, 0), self.peers["c"])
            for half in range(2):
                own, got = self.ref("own" + "xy"[half]), self.ref("got" + "xy"[half])
                chunk = self.chunk(half, k)
                own[chunk] = own[chunk] + got[chunk]
                if k:
                    for part in FAR_4 + (0,):
                        self.second_copy(half, k, part).start()

    def start_third(self):
        for k in FAR_4 + (0,):
            arrival(self.ref("bx").at[pl.ds(0, 2)], self.ref("in2").at[k], self.sent(1, 0), self.peers["c"])
            for half in range(2):
                name, part = "xy"[half], self.chunk(1 - half, k)
                landed, own = self.ref("b" + name).at[part], self.ref("own" + name)
                self.ref("c" + name)[part] = own[self.pos[half], part] + landed[0] + landed[1] + landed[2]
                if k:
                    self.third_copy(half, k).start()

    def start_last(self):
        zs = self.ref("zs")
        for half in range(2):
            landed = self.ref("d" + "xy"[half])
            arrival(landed, self.ref("in3").at[half], self.sent(2, half), self.peers["c"])
            total = self.ref("c" + "xy"[half])[self.pos[1 - half]] + landed[0] + landed[1] + landed[2]
            zs[8 * half : 8 * half + 8] = total.reshape(8, 4, 128)
        for d in FAR_16:
            self.last_copy(d).start()

    def finish(self, out, scale):
        zb = self.ref("zb")
        arrival(zb, self.ref("in3").at[2], self.sent(3, 0), self.peers["c"])
        out[...] = (self.ref("zs")[self.pos[2]] + sum(zb[d - 1] for d in range(1, ZS))) * scale

    def drain(self):
        spare = self.ref("in3").at[0]
        for half, name in enumerate("xy"):
            departure(self.ref("send" + name), self.sent(0, half), spare, self.peers["c"])
            departure(self.ref("b" + name), self.sent(1, half), spare, self.peers["c"])
            departure(self.ref("d" + name), self.sent(2, half), spare, self.peers["c"])
        departure(self.ref("zb"), self.sent(3, 0), spare, self.peers["c"])


def reduce_scratch(tag):
    dma = pltpu.SemaphoreType.DMA
    return {
        "x" + tag: pltpu.VMEM((2, YS, TILES, 8, 128), F32),
        "out" + tag: pltpu.VMEM((2, YS, TILES, 8, 128), F32),
        "bufc" + tag: pltpu.VMEM((YS, TILES, 8, 128), F32),
        "accc" + tag: pltpu.VMEM((YS, TILES, 8, 128), F32),
        "bufy" + tag: pltpu.VMEM((TILES, YS - 1, 8, 128), F32),
        "accy" + tag: pltpu.VMEM((TILES, 8, 128), F32),
        "bufz" + tag: pltpu.VMEM((ZS - 1, 8, 128), F32),
        "sent" + tag: dma((7,)),
        "cross" + tag: dma((1,)),
        "corein" + tag: dma((YS,)),
        "yin" + tag: dma((TILES,)),
        "zin" + tag: dma((1,)),
        "zout" + tag: dma((TILES,)),
        "yout" + tag: dma((YS - 1,)),
        "coreout" + tag: dma((1,)),
    }


def scatter_scratch(tag):
    dma = pltpu.SemaphoreType.DMA
    names = {}
    for axis in ("x", "y"):
        for kind in ("send", "got", "own"):
            names[kind + axis + tag] = pltpu.VMEM((4, 4, 32, 128), F32)
        names["b" + axis + tag] = pltpu.VMEM((4, 3, 32, 128), F32)
        names["c" + axis + tag] = pltpu.VMEM((4, 32, 128), F32)
        names["d" + axis + tag] = pltpu.VMEM((3, 32, 128), F32)
    names["zs" + tag] = pltpu.VMEM((ZS, 4, 128), F32)
    names["zb" + tag] = pltpu.VMEM((ZS - 1, 4, 128), F32)
    names["sent" + tag] = dma((7,))
    names["in1" + tag] = dma((4,))
    names["in2" + tag] = dma((4,))
    names["in3" + tag] = dma((3,))
    return names


def scratch():
    full = pltpu.VMEM((ROWS, D), F32)
    half = pltpu.VMEM((ROWS, D), BF16)
    names = {n: full for n in ("uq", "uk", "fq", "fk", "att", "rden", "gnum", "gden", "wtd", "gin")}
    names.update({n: half for n in ("fqh", "fql", "fkh", "fkl", "vh", "vl", "gnh", "gnl", "gq", "gk", "gv")})
    names["gh"] = pltpu.VMEM((ROWS, F), F32)
    names["turn"] = pltpu.VMEM((2, QUAD, ROWS), BF16)
    names["ones"] = pltpu.VMEM((QUAD, QUAD), BF16)
    names["ph"] = pltpu.VMEM((2, QUAD, QUAD), BF16)
    names["pl"] = pltpu.VMEM((2, QUAD, QUAD), BF16)
    for n in ("sh", "sl", "gsh", "gsl"):
        names[n] = pltpu.VMEM((T, 2, QUAD, QUAD), BF16)
    names.update(reduce_scratch("_1"))
    names.update(reduce_scratch("_2"))
    for tag in ("_q", "_k", "_v"):
        names.update(scatter_scratch(tag))
    for n, (shape, kind) in STAGED.items():
        names["in_" + n] = pltpu.VMEM(shape, kind)
    names["fetch"] = pltpu.SemaphoreType.DMA((len(STAGED) + 1,))
    names["gout"] = pltpu.VMEM((T, N, D), BF16)
    return names


def kernel(
    scale, x_hbm, cot_hbm, wq_hbm, wk_hbm, wv_hbm, up_hbm, down_hbm, proj_hbm, live_ref,
    gin_ref, oq_ref, ok_ref, ov_ref, *rest,
):
    r = dict(zip(scratch().keys(), rest))
    sources = dict(
        x=x_hbm, cot=cot_hbm, wq=wq_hbm, wk=wk_hbm, wv=wv_hbm, up=up_hbm, down=down_hbm, proj=proj_hbm
    )
    fetches = {
        n: pltpu.make_async_copy(sources[n], r["in_" + n], r["fetch"].at[i]) for i, n in enumerate(STAGED)
    }
    start([fetches[n] for n in ("x", "wk", "proj", "wv")])

    def fetched(n):
        fetches[n].wait()
        return r["in_" + n]

    s = lax.axis_index("sensor")
    x, y, z, c = lax.axis_index("step"), s // (2 * ZS), lax.rem(s // 2, ZS), lax.rem(s, 2)
    pos = (x, y, z, c)
    peers = {
        "c": at(x, y, z, 1 - c),
        "y": [at(x, lax.rem(y + d, YS), z, c) for d in range(1, YS)],
        "x": [at(lax.rem(x + d, XS), y, z, c) for d in range(1, XS)],
        "z": [at(x, y, lax.rem(z + d, ZS), c) for d in range(1, ZS)],
    }
    peers["far"] = at(x, lax.rem(y + 2, YS), z, 1 - c)
    everyone = [peers["c"], peers["far"]] + peers["y"] + peers["x"] + peers["z"]
    barrier = pltpu.get_barrier_semaphore()
    for target in everyone:
        pl.semaphore_signal(barrier, inc=1, device_id=target, device_id_type=MESH)

    row_id = lax.rem(lax.broadcasted_iota(jnp.int32, (ROWS, 1), 0), N)
    quads = [pl.ds(QUAD * q, QUAD) for q in range(2)]
    moments = [pl.ds(N * t, N) for t in range(T)]

    same = lax.broadcasted_iota(jnp.int32, (QUAD, QUAD), 0) // E == lax.broadcasted_iota(jnp.int32, (QUAD, QUAD), 1) // E
    r["ones"][...] = jnp.where(same, 1.0, 0.0).astype(BF16)
    ones = r["ones"]
    zero = jnp.zeros((E, E), F32)
    rows = fetched("x")[...].reshape(ROWS, D)
    r["uk"][...] = dot(rows, fetched("wk")[...]) * FACTOR
    start([fetches[n] for n in ("wq", "cot", "down", "up")])
    proj_ref = fetched("proj")
    for q in range(2):
        lines = []
        for k in range(4):
            parts = [zero] * 4
            parts[k] = proj_ref[4 * q + k]
            lines.append(jnp.concatenate(parts, axis=1))
        r["ph"][q], r["pl"][q] = split(jnp.concatenate(lines, axis=0))

    def features(u_ref, q):
        u = u_ref[:, quads[q]]
        exponent = dot3(dot, split(u), (r["ph"][q], r["pl"][q])) - 0.5 * head_sum(u * u, ones[...])
        return jnp.exp(exponent) * (E ** -0.5)

    def feature_back(weighted, u, q):
        back = dot3(dot_nt, split(weighted), (r["ph"][q], r["pl"][q])) - u * head_sum(weighted, ones[...])
        return (back * FACTOR).astype(BF16)

    r["vh"][...], r["vl"][...] = split(dot(rows, fetched("wv")[...]))
    valid = row_id < live_ref[0]
    for q in range(2):
        fk = jnp.where(valid, features(r["uk"], q), 0.0)
        r["fk"][:, quads[q]] = fk
        r["fkh"][:, quads[q]], r["fkl"][:, quads[q]] = split(fk)

    def outer(a, b, t, q):
        (ah, al), (bh, bl) = a, b
        here = moments[t], quads[q]
        left = jnp.concatenate([ah[here], al[here], ah[here]], axis=0)
        right = jnp.concatenate([bh[here], bh[here], bl[here]], axis=0)
        return dot_tn(left, right)

    first, second = Reduce(pos, peers, r, "_1"), Reduce(pos, peers, r, "_2")
    for ref in (first.x, second.x):
        ref[:, :, TILES - 1] = jnp.zeros((2, YS, 8, 128), F32)
    for t in range(T):
        for q in range(2):
            put_blocks(first.x, t, q, outer((r["fkh"], r["fkl"]), (r["vh"], r["vl"]), t, q))
        total = jnp.sum(r["fk"][moments[t], :], axis=0, keepdims=True)
        for p in range(PAIRS):
            put_row(first.x, t, p, total[:, 128 * p : 128 * p + 128])

    pl.semaphore_wait(barrier, len(everyone))
    first.start_core()
    wq_ref = fetched("wq")
    r["uq"][...] = dot(rows, wq_ref[...]) * FACTOR
    first.start_y()
    for q in range(2):
        fq = features(r["uq"], q)
        r["fq"][:, quads[q]] = fq
        r["fqh"][:, quads[q]], r["fql"][:, quads[q]] = split(fq)
    first.start_z()
    masked = jnp.where(valid, fetched("cot")[...].reshape(ROWS, D), jnp.zeros((), BF16))
    r["gh"][...] = dot_nt(masked, fetched("down")[...])
    up_ref = fetched("up")
    for n in ("sh", "sl", "gsh", "gsl"):
        r[n][...] = jnp.zeros_like(r[n])
    first.start_z_back()
    line = lax.broadcasted_iota(jnp.int32, (QUAD, D), 0)
    column = lax.broadcasted_iota(jnp.int32, (QUAD, D), 1)
    for k in range(2):
        source = (line // 64) * 128 + lax.rem(line // 4, ZS) * 8 + 4 * k + lax.rem(line, 4)
        pick = jnp.where(source == column, 1.0, 0.0).astype(BF16)
        r["turn"][k] = dot_nt(pick, rows).astype(BF16)
    first.start_y_back()
    first.start_core_back()
    first.finish()

    for t in range(T):
        for q in range(2):
            here = moments[t], quads[q]
            get_blocks(first.out, t, q, r["sh"], r["sl"])
            numer = dot3(dot, (r["fqh"][here], r["fql"][here]), (r["sh"][t, q], r["sl"][t, q]))
            inverse = 1.0 / head_sum(r["fq"][here] * get_row(first.out, t, q), ones[...])
            r["rden"][here] = inverse
            r["att"][here] = numer * inverse
    att = r["att"][...]
    rms_inverse = 1.0 / jnp.sqrt(jnp.mean(att * att, axis=1, keepdims=True) + 1e-06)
    normed = att * rms_inverse
    pre = dot(normed.astype(BF16), up_ref[...])
    grad_pre = (r["gh"][...] * gelu_slope(pre)).astype(BF16)
    grad_normed = dot_nt(grad_pre, up_ref[...])
    mean = jnp.mean(grad_normed * normed, axis=1, keepdims=True)
    grad_att = (grad_normed - normed * mean) * rms_inverse
    for q in range(2):
        ga = grad_att[:, QUAD * q : QUAD * q + QUAD]
        inverse = r["rden"][:, quads[q]]
        gnum = ga * inverse
        r["gnum"][:, quads[q]] = gnum
        r["gnh"][:, quads[q]], r["gnl"][:, quads[q]] = split(gnum)
        r["gden"][:, quads[q]] = -head_sum(ga * r["att"][:, quads[q]], ones[...]) * inverse
    for t in range(T):
        for q in range(2):
            put_blocks(second.x, t, q, outer((r["fqh"], r["fql"]), (r["gnh"], r["gnl"]), t, q))
        total = jnp.sum(r["fq"][moments[t], :] * r["gden"][moments[t], :], axis=0, keepdims=True)
        for p in range(PAIRS):
            put_row(second.x, t, p, total[:, 128 * p : 128 * p + 128])

    second.start_core()
    for t in range(T):
        for q in range(2):
            here = moments[t], quads[q]
            gfq = dot3(dot_nt, (r["gnh"][here], r["gnl"][here]), (r["sh"][t, q], r["sl"][t, q]))
            gfq = gfq + r["gden"][here] * get_row(first.out, t, q)
            r["wtd"][here] = gfq * r["fq"][here]
    second.start_y()
    for q in range(2):
        r["gq"][:, quads[q]] = feature_back(r["wtd"][:, quads[q]], r["uq"][:, quads[q]], q)
    job_q, job_k, job_v = (Scatter(pos, peers, r, tag) for tag in ("_q", "_k", "_v"))
    job_q.put("send", dot(r["turn"][1 - c], r["gq"][...]))
    second.start_z()
    job_q.start_core()
    job_q.put("own", dot(r["turn"][c], r["gq"][...]))
    job_q.start_second()
    r["gin"][...] = dot_nt(r["gq"][...], wq_ref[...])
    second.start_z_back()
    second.start_y_back()
    job_q.start_third()
    second.start_core_back()
    second.finish()

    for t in range(T):
        for q in range(2):
            here = moments[t], quads[q]
            get_blocks(second.out, t, q, r["gsh"], r["gsl"])
            blocks = (r["gsh"][t, q], r["gsl"][t, q])
            r["gv"][here] = dot3(dot, (r["fkh"][here], r["fkl"][here]), blocks).astype(BF16)
    job_v.put("send", dot(r["turn"][1 - c], r["gv"][...]))
    job_v.start_core()
    for t in range(T):
        for q in range(2):
            here = moments[t], quads[q]
            blocks = (r["gsh"][t, q], r["gsl"][t, q])
            gfk = dot3(dot_nt, (r["vh"][here], r["vl"][here]), blocks) + get_row(second.out, t, q)
            r["wtd"][here] = gfk * r["fk"][here]
    for q in range(2):
        r["gk"][:, quads[q]] = feature_back(r["wtd"][:, quads[q]], r["uk"][:, quads[q]], q)
    job_k.put("send", dot(r["turn"][1 - c], r["gk"][...]))
    job_k.start_core()
    job_q.start_last()
    job_v.put("own", dot(r["turn"][c], r["gv"][...]))
    job_v.start_second()
    job_k.put("own", dot(r["turn"][c], r["gk"][...]))
    job_k.start_second()
    total = r["gin"][...] + dot_nt(r["gk"][...], r["in_wk"][...]) + dot_nt(r["gv"][...], r["in_wv"][...])
    r["gout"][...] = total.astype(BF16).reshape(T, N, D)
    leave = pltpu.make_async_copy(r["gout"], gin_ref, r["fetch"].at[len(STAGED)])
    leave.start()
    job_v.start_third()
    job_k.start_third()
    job_v.start_last()
    job_k.start_last()
    job_q.finish(oq_ref, scale)
    job_v.finish(ov_ref, scale)
    job_k.finish(ok_ref, scale)
    for job in (first, second, job_q, job_k, job_v):
        job.drain()
    leave.wait()


def hand_on(*refs):
    for source, target in zip(refs[:4], refs[4:]):
        target[...] = source[...]


def shards(inputs, cotangent, w_query, w_key, w_value, w_up, w_down, feature_proj, live_count):
    total_rows = T * XS * N * YS * ZS * 2
    piece = jax.ShapeDtypeStruct((4, 128), F32)
    shapes = (jax.ShapeDtypeStruct((T, N, D), BF16), piece, piece, piece)
    results = pl.pallas_call(
        functools.partial(kernel, 1.0 / math.sqrt(total_rows)),
        out_shape=shapes,
        in_specs=[ANY] * 8 + [SM],
        out_specs=(ANY, VM, VM, VM),
        scratch_shapes=list(scratch().values()),
        compiler_params=pltpu.CompilerParams(collective_id=0, has_side_effects=True, vmem_limit_bytes=56 << 20),
    )(inputs, cotangent, w_query, w_key, w_value, w_up, w_down, feature_proj, live_count)
    return pl.pallas_call(
        hand_on,
        out_shape=shapes,
        in_specs=[VM] * 4,
        out_specs=(VM,) * 4,
    )(*results)


def solution(mesh):
    placed = (P("step", "sensor", None),) * 2 + (P(),) * 6 + (P("sensor"),)
    return jax.shard_map(
        shards,
        mesh=mesh,
        in_specs=placed,
        out_specs=(P("step", "sensor", None),) + (P("sensor", "step"),) * 3,
        check_vma=False,
    )
```

```python
import functools
import math

import jax
import jax.numpy as jnp
from jax import lax
from jax.experimental import pallas as pl
from jax.experimental.pallas import tpu as pltpu
from jax.sharding import PartitionSpec as P

MESH = pl.DeviceIdType.MESH
VM = pl.BlockSpec(memory_space=pltpu.VMEM)
SM = pl.BlockSpec(memory_space=pltpu.SMEM)
ANY = pl.BlockSpec(memory_space=pl.ANY)
F32, BF16 = jnp.float32, jnp.bfloat16
YS, ZS, XS = 4, 16, 4
T, N, D, F, H, E = 3, 64, 512, 256, 8, 64
ROWS = T * N
PAIRS = H // 2
TILES = 13
QUAD = 256
FACTOR = E ** (-0.25)
STAGED = {
    "x": ((T, N, D), BF16),
    "wk": ((D, D), BF16),
    "proj": ((H, E, E), F32),
    "wv": ((D, D), BF16),
    "wq": ((D, D), BF16),
    "cot": ((T, N, D), BF16),
    "down": ((F, D), BF16),
    "up": ((D, F), BF16),
}
FAR_4 = (2, 1, 3)
FAR_16 = (8, 7, 9, 6, 10, 5, 11, 4, 12, 3, 13, 2, 14, 1, 15)


def at(x, y, z, c):
    return ((y * ZS + z) * 2 + c, x)


def send(src, dst, ssem, rsem, target):
    return pltpu.make_async_remote_copy(
        src_ref=src, dst_ref=dst, send_sem=ssem, recv_sem=rsem, device_id=target, device_id_type=MESH
    )


def start(copies):
    for copy in copies:
        copy.start()


def wait(copies):
    for copy in copies:
        copy.wait()


def arrival(ref, landed, sent, peer):
    send(ref, ref, sent, landed, peer).wait_recv()


def departure(ref, sent, landed, peer):
    send(ref, ref, sent, landed, peer).wait_send()


def dot(a, b):
    return lax.dot_general(a, b, (((1,), (0,)), ((), ())), preferred_element_type=F32)


def dot_nt(a, b):
    return lax.dot_general(a, b, (((1,), (1,)), ((), ())), preferred_element_type=F32)


def dot_tn(a, b):
    return lax.dot_general(a, b, (((0,), (0,)), ((), ())), preferred_element_type=F32)


def split(value):
    high = value.astype(BF16)
    return high, (value - high.astype(F32)).astype(BF16)


def dot3(product, a, b):
    return product(a[0], b[0]) + product(a[1], b[0]) + product(a[0], b[1])


def head_sum(value, ones):
    high, low = split(value)
    return dot(high, ones) + dot(low, ones)


def gelu_slope(v):
    k = math.sqrt(2 / math.pi)
    th = jnp.tanh(k * (v + 0.044715 * v * v * v))
    return 0.5 * (1.0 + th) + 0.5 * v * (1.0 - th * th) * (k * (1.0 + 3 * 0.044715 * v * v))


class Reduce:
    def __init__(self, pos, peers, r, tag):
        self.pos, self.peers = pos, peers
        self.x, self.out = r["x" + tag], r["out" + tag]
        self.buf_c, self.acc_c = r["bufc" + tag], r["accc" + tag]
        self.buf_y, self.acc_y, self.buf_z = r["bufy" + tag], r["accy" + tag], r["bufz" + tag]
        self.sent, self.core_in, self.y_in = r["sent" + tag], r["corein" + tag], r["yin" + tag]
        self.z_in, self.z_out, self.y_out, self.core_out = r["zin" + tag], r["zout" + tag], r["yout" + tag], r["coreout" + tag]
        self.cross = r["cross" + tag]

    def core_down(self, k):
        chunk = lax.rem(self.pos[1] + k, YS)
        source = self.x.at[1 - self.pos[3], chunk]
        return send(source, self.buf_c.at[chunk], self.sent.at[0], self.core_in.at[k], self.peers["c"])

    def y_down(self, d, tile):
        chunk = lax.rem(self.pos[1] + d, YS)
        target = self.buf_y.at[tile, d - 1]
        return send(self.acc_c.at[chunk, tile], target, self.sent.at[1], self.y_in.at[tile], self.peers["y"][d - 1])

    def z_down(self, d, tile):
        return send(self.acc_y.at[tile], self.buf_z.at[d - 1], self.sent.at[2], self.z_in.at[0], self.peers["z"][d - 1])

    def z_up(self, d, tile):
        piece = self.out.at[self.pos[3], self.pos[1], tile]
        return send(piece, piece, self.sent.at[3], self.z_out.at[tile], self.peers["z"][d - 1])

    def y_up(self, d, piece):
        return send(piece, piece, self.sent.at[4], self.y_out.at[0], self.peers["y"][d - 1])

    def cross_up(self, d, piece):
        return send(piece, piece, self.sent.at[6], self.cross.at[0], self.peers["cross"][d - 1])

    def core_up(self, group):
        piece = self.out.at[self.pos[3], group]
        return send(piece, piece, self.sent.at[5], self.core_out.at[0], self.peers["c"])

    def start_core(self):
        for k in FAR_4 + (0,):
            self.core_down(k).start()

    def start_y(self):
        _, y, z, c = self.pos
        for k in FAR_4 + (0,):
            self.core_down(k).wait_recv()
            chunk = lax.rem(y + k, YS)
            self.acc_c[chunk] = self.x[c, chunk] + self.buf_c[chunk]
            if k:
                for d in FAR_16 + (0,):
                    tile = lax.rem(z + d, ZS)

                    @pl.when(tile < TILES)
                    def _():
                        self.y_down(k, tile).start()

    def start_z(self):
        _, y, z, _ = self.pos
        for d in FAR_16 + (0,):
            tile = lax.rem(z + d, ZS)

            @pl.when(tile < TILES)
            def _():
                landed = self.buf_y.at[tile]
                arrival(landed, self.y_in.at[tile], self.sent.at[1], self.peers["c"])
                self.acc_y[tile] = self.acc_c[y, tile] + landed[0] + landed[1] + landed[2]
                if d:
                    self.z_down(d, tile).start()

    def start_z_back(self):
        _, y, z, c = self.pos

        @pl.when(z < TILES)
        def _():
            arrival(self.buf_z, self.z_in.at[0], self.sent.at[2], self.peers["c"])
            self.out[c, y, z] = self.acc_y[z] + sum(self.buf_z[d - 1] for d in range(1, ZS))
            for d in FAR_16:
                self.z_up(d, z).start()
            for d in FAR_4:
                self.y_up(d, self.out.at[c, y, z]).start()
                self.cross_up(d, self.out.at[c, y, z]).start()

    def start_y_back(self):
        _, y, z, c = self.pos
        for d in FAR_16[::-1]:
            source = lax.rem(z + ZS - d, ZS)

            @pl.when(source < TILES)
            def _():
                self.z_up(d, source).wait_recv()
                for e in FAR_4:
                    self.y_up(e, self.out.at[c, y, source]).start()
                    self.cross_up(e, self.out.at[c, y, source]).start()

    def start_core_back(self):
        _, y, _, c = self.pos
        self.core_up(y).start()

    def finish(self):
        _, y, _, c = self.pos
        peer = self.peers["c"]
        arrival(self.buf_y, self.y_out.at[0], self.sent.at[4], peer)
        arrival(self.buf_y, self.cross.at[0], self.sent.at[6], peer)
        arrival(self.out.at[1 - c, y], self.core_out.at[0], self.sent.at[5], peer)

    def drain(self):
        z, peer = self.pos[2], self.peers["c"]
        departure(self.buf_c, self.sent.at[0], self.core_in.at[0], peer)
        departure(self.buf_y, self.sent.at[1], self.y_in.at[0], peer)
        departure(self.buf_y, self.sent.at[4], self.y_in.at[0], peer)
        departure(self.acc_y, self.sent.at[5], self.core_in.at[0], peer)
        departure(self.buf_y, self.sent.at[6], self.core_in.at[0], peer)

        @pl.when(z < TILES)
        def _():
            departure(self.acc_y.at[pl.ds(0, TILES - 1)], self.sent.at[2], self.z_in.at[0], peer)
            departure(self.buf_z, self.sent.at[3], self.z_in.at[0], peer)

        @pl.when(z >= TILES)
        def _():
            departure(self.acc_y, self.sent.at[2], self.z_in.at[0], peer)


def tile_place(tile):
    group, slot = divmod(tile, 12)
    return group // YS, group % YS, slot


def put_blocks(ref, moment, quad, result):
    first = lax.broadcasted_iota(jnp.int32, (E, 128), 1) < E
    for j in range(2):
        part = result[128 * j : 128 * j + 128, 128 * j : 128 * j + 128]
        block = jnp.where(first, part[0:E], part[E:128]).reshape(8, 8, 128)
        for half in range(2):
            c, y, slot = tile_place((moment * PAIRS + 2 * quad + j) * 8 + 4 * half)
            ref[c, y, pl.ds(slot, 4)] = block[4 * half : 4 * half + 4]


def row_place(moment, pair):
    row = moment * PAIRS + pair
    group = row // 2
    return group // YS, group % YS, row % 2


def put_row(ref, moment, pair, row):
    c, y, k = row_place(moment, pair)
    ref[c, y, TILES - 1, pl.ds(k, 1)] = row


def get_row(ref, moment, quad):
    rows = []
    for j in range(2):
        c, y, k = row_place(moment, 2 * quad + j)
        rows.append(ref[c, y, TILES - 1, pl.ds(k, 1)])
    return jnp.concatenate(rows, axis=1)


def get_blocks(ref, moment, quad, high_ref, low_ref):
    first = lax.broadcasted_iota(jnp.int32, (E, 128), 1) < E
    for j in range(2):
        halves = []
        for half in range(2):
            c, y, slot = tile_place((moment * PAIRS + 2 * quad + j) * 8 + 4 * half)
            halves.append(ref[c, y, pl.ds(slot, 4)].reshape(32, 128))
        block = jnp.concatenate(halves, axis=0)
        for k, kept in enumerate((jnp.where(first, block, 0.0), jnp.where(first, 0.0, block))):
            high, low = split(kept)
            here = pl.ds(128 * j + E * k, E), pl.ds(128 * j, 128)
            high_ref[moment, quad, here[0], here[1]] = high
            low_ref[moment, quad, here[0], here[1]] = low


class Scatter:
    def __init__(self, pos, peers, r, tag):
        self.pos, self.peers, self.r, self.tag = pos, peers, r, tag

    def ref(self, name):
        return self.r[name + self.tag]

    def put(self, name, result):
        xf, yf = self.ref(name + "x"), self.ref(name + "y")
        for y in range(YS):
            for x in range(XS):
                block = result[64 * y : 64 * y + 64, 128 * x : 128 * x + 128]
                xf[x, y] = block[0:32]
                yf[y, x] = block[32:64]

    def chunk(self, half, k):
        return lax.rem(self.pos[half] + k, 4)

    def sent(self, phase, half):
        return self.ref("sent").at[2 * phase + half]

    def core_copy(self, half, k):
        name, chunk = "xy"[half], self.chunk(half, k)
        return send(
            self.ref("send" + name).at[chunk], self.ref("got" + name).at[chunk], self.sent(0, half),
            self.ref("in1").at[k], self.peers["c"],
        )

    def second_copy(self, half, d, k):
        name, part = "xy"[half], self.chunk(1 - half, k)
        return send(
            self.ref("own" + name).at[self.chunk(half, d), part], self.ref("b" + name).at[part, d - 1],
            self.sent(1, half), self.ref("in2").at[k], self.peers[name][d - 1],
        )

    def third_copy(self, half, d):
        name, other = "xy"[half], "yx"[half]
        return send(
            self.ref("c" + name).at[self.chunk(1 - half, d)], self.ref("d" + name).at[d - 1],
            self.sent(2, half), self.ref("in3").at[half], self.peers[other][d - 1],
        )

    def last_copy(self, d):
        return send(
            self.ref("zs").at[lax.rem(self.pos[2] + d, ZS)], self.ref("zb").at[d - 1],
            self.sent(3, 0), self.ref("in3").at[2], self.peers["z"][d - 1],
        )

    def start_core(self):
        for k in FAR_4 + (0,):
            for half in range(2):
                self.core_copy(half, k).start()

    def start_second(self):
        for k in FAR_4 + (0,):
            arrival(self.ref("gotx").at[pl.ds(0, 2)], self.ref("in1").at[k], self.sent(0, 0), self.peers["c"])
            for half in range(2):
                own, got = self.ref("own" + "xy"[half]), self.ref("got" + "xy"[half])
                chunk = self.chunk(half, k)
                own[chunk] = own[chunk] + got[chunk]
                if k:
                    for part in FAR_4 + (0,):
                        self.second_copy(half, k, part).start()

    def start_third(self):
        for k in FAR_4 + (0,):
            arrival(self.ref("bx").at[pl.ds(0, 2)], self.ref("in2").at[k], self.sent(1, 0), self.peers["c"])
            for half in range(2):
                name, part = "xy"[half], self.chunk(1 - half, k)
                landed, own = self.ref("b" + name).at[part], self.ref("own" + name)
                self.ref("c" + name)[part] = own[self.pos[half], part] + landed[0] + landed[1] + landed[2]
                if k:
                    self.third_copy(half, k).start()

    def start_last(self):
        zs = self.ref("zs")
        for half in range(2):
            landed = self.ref("d" + "xy"[half])
            arrival(landed, self.ref("in3").at[half], self.sent(2, half), self.peers["c"])
            total = self.ref("c" + "xy"[half])[self.pos[1 - half]] + landed[0] + landed[1] + landed[2]
            zs[8 * half : 8 * half + 8] = total.reshape(8, 4, 128)
        for d in FAR_16:
            self.last_copy(d).start()

    def finish(self, out, scale):
        zb = self.ref("zb")
        arrival(zb, self.ref("in3").at[2], self.sent(3, 0), self.peers["c"])
        out[...] = (self.ref("zs")[self.pos[2]] + sum(zb[d - 1] for d in range(1, ZS))) * scale

    def drain(self):
        spare = self.ref("in3").at[0]
        for half, name in enumerate("xy"):
            departure(self.ref("send" + name), self.sent(0, half), spare, self.peers["c"])
            departure(self.ref("b" + name), self.sent(1, half), spare, self.peers["c"])
            departure(self.ref("d" + name), self.sent(2, half), spare, self.peers["c"])
        departure(self.ref("zb"), self.sent(3, 0), spare, self.peers["c"])


def reduce_scratch(tag):
    dma = pltpu.SemaphoreType.DMA
    return {
        "x" + tag: pltpu.VMEM((2, YS, TILES, 8, 128), F32),
        "out" + tag: pltpu.VMEM((2, YS, TILES, 8, 128), F32),
        "bufc" + tag: pltpu.VMEM((YS, TILES, 8, 128), F32),
        "accc" + tag: pltpu.VMEM((YS, TILES, 8, 128), F32),
        "bufy" + tag: pltpu.VMEM((TILES, YS - 1, 8, 128), F32),
        "accy" + tag: pltpu.VMEM((TILES, 8, 128), F32),
        "bufz" + tag: pltpu.VMEM((ZS - 1, 8, 128), F32),
        "sent" + tag: dma((7,)),
        "cross" + tag: dma((1,)),
        "corein" + tag: dma((YS,)),
        "yin" + tag: dma((TILES,)),
        "zin" + tag: dma((1,)),
        "zout" + tag: dma((TILES,)),
        "yout" + tag: dma((1,)),
        "coreout" + tag: dma((1,)),
    }


def scatter_scratch(tag):
    dma = pltpu.SemaphoreType.DMA
    names = {}
    for axis in ("x", "y"):
        for kind in ("send", "got", "own"):
            names[kind + axis + tag] = pltpu.VMEM((4, 4, 32, 128), F32)
        names["b" + axis + tag] = pltpu.VMEM((4, 3, 32, 128), F32)
        names["c" + axis + tag] = pltpu.VMEM((4, 32, 128), F32)
        names["d" + axis + tag] = pltpu.VMEM((3, 32, 128), F32)
    names["zs" + tag] = pltpu.VMEM((ZS, 4, 128), F32)
    names["zb" + tag] = pltpu.VMEM((ZS - 1, 4, 128), F32)
    names["sent" + tag] = dma((7,))
    names["in1" + tag] = dma((4,))
    names["in2" + tag] = dma((4,))
    names["in3" + tag] = dma((3,))
    return names


def scratch():
    full = pltpu.VMEM((ROWS, D), F32)
    half = pltpu.VMEM((ROWS, D), BF16)
    names = {n: full for n in ("uq", "uk", "fq", "fk", "att", "rden", "gnum", "gden", "wtd", "gin")}
    names.update({n: half for n in ("fqh", "fql", "fkh", "fkl", "vh", "vl", "gnh", "gnl", "gq", "gk", "gv")})
    names["gh"] = pltpu.VMEM((ROWS, F), F32)
    names["turn"] = pltpu.VMEM((2, QUAD, ROWS), BF16)
    names["ones"] = pltpu.VMEM((QUAD, QUAD), BF16)
    names["ph"] = pltpu.VMEM((2, QUAD, QUAD), BF16)
    names["pl"] = pltpu.VMEM((2, QUAD, QUAD), BF16)
    for n in ("sh", "sl", "gsh", "gsl"):
        names[n] = pltpu.VMEM((T, 2, QUAD, QUAD), BF16)
    names.update(reduce_scratch("_1"))
    names.update(reduce_scratch("_2"))
    for tag in ("_q", "_k", "_v"):
        names.update(scatter_scratch(tag))
    for n, (shape, kind) in STAGED.items():
        names["in_" + n] = pltpu.VMEM(shape, kind)
    names["fetch"] = pltpu.SemaphoreType.DMA((len(STAGED) + 1,))
    names["gout"] = pltpu.VMEM((T, N, D), BF16)
    return names


def kernel(
    scale, x_hbm, cot_hbm, wq_hbm, wk_hbm, wv_hbm, up_hbm, down_hbm, proj_hbm, live_ref,
    gin_ref, oq_ref, ok_ref, ov_ref, *rest,
):
    r = dict(zip(scratch().keys(), rest))
    sources = dict(
        x=x_hbm, cot=cot_hbm, wq=wq_hbm, wk=wk_hbm, wv=wv_hbm, up=up_hbm, down=down_hbm, proj=proj_hbm
    )
    fetches = {
        n: pltpu.make_async_copy(sources[n], r["in_" + n], r["fetch"].at[i]) for i, n in enumerate(STAGED)
    }
    start([fetches[n] for n in ("x", "wk", "proj", "wv")])

    def fetched(n):
        fetches[n].wait()
        return r["in_" + n]

    s = lax.axis_index("sensor")
    x, y, z, c = lax.axis_index("step"), s // (2 * ZS), lax.rem(s // 2, ZS), lax.rem(s, 2)
    pos = (x, y, z, c)
    peers = {
        "c": at(x, y, z, 1 - c),
        "y": [at(x, lax.rem(y + d, YS), z, c) for d in range(1, YS)],
        "x": [at(lax.rem(x + d, XS), y, z, c) for d in range(1, XS)],
        "z": [at(x, y, lax.rem(z + d, ZS), c) for d in range(1, ZS)],
    }
    peers["cross"] = [at(x, lax.rem(y + d, YS), z, 1 - c) for d in range(1, YS)]
    everyone = [peers["c"]] + peers["cross"] + peers["y"] + peers["x"] + peers["z"]
    barrier = pltpu.get_barrier_semaphore()
    for target in everyone:
        pl.semaphore_signal(barrier, inc=1, device_id=target, device_id_type=MESH)

    row_id = lax.rem(lax.broadcasted_iota(jnp.int32, (ROWS, 1), 0), N)
    quads = [pl.ds(QUAD * q, QUAD) for q in range(2)]
    moments = [pl.ds(N * t, N) for t in range(T)]

    same = lax.broadcasted_iota(jnp.int32, (QUAD, QUAD), 0) // E == lax.broadcasted_iota(jnp.int32, (QUAD, QUAD), 1) // E
    r["ones"][...] = jnp.where(same, 1.0, 0.0).astype(BF16)
    ones = r["ones"]
    zero = jnp.zeros((E, E), F32)
    rows = fetched("x")[...].reshape(ROWS, D)
    r["uk"][...] = dot(rows, fetched("wk")[...]) * FACTOR
    start([fetches[n] for n in ("wq", "cot", "down", "up")])
    proj_ref = fetched("proj")
    for q in range(2):
        lines = []
        for k in range(4):
            parts = [zero] * 4
            parts[k] = proj_ref[4 * q + k]
            lines.append(jnp.concatenate(parts, axis=1))
        r["ph"][q], r["pl"][q] = split(jnp.concatenate(lines, axis=0))

    def features(u_ref, q):
        u = u_ref[:, quads[q]]
        exponent = dot3(dot, split(u), (r["ph"][q], r["pl"][q])) - 0.5 * head_sum(u * u, ones[...])
        return jnp.exp(exponent) * (E ** -0.5)

    def feature_back(weighted, u, q):
        back = dot3(dot_nt, split(weighted), (r["ph"][q], r["pl"][q])) - u * head_sum(weighted, ones[...])
        return (back * FACTOR).astype(BF16)

    r["vh"][...], r["vl"][...] = split(dot(rows, fetched("wv")[...]))
    valid = row_id < live_ref[0]
    for q in range(2):
        fk = jnp.where(valid, features(r["uk"], q), 0.0)
        r["fk"][:, quads[q]] = fk
        r["fkh"][:, quads[q]], r["fkl"][:, quads[q]] = split(fk)

    def outer(a, b, t, q):
        (ah, al), (bh, bl) = a, b
        here = moments[t], quads[q]
        left = jnp.concatenate([ah[here], al[here], ah[here]], axis=0)
        right = jnp.concatenate([bh[here], bh[here], bl[here]], axis=0)
        return dot_tn(left, right)

    first, second = Reduce(pos, peers, r, "_1"), Reduce(pos, peers, r, "_2")
    for ref in (first.x, second.x):
        ref[:, :, TILES - 1] = jnp.zeros((2, YS, 8, 128), F32)
    for t in range(T):
        for q in range(2):
            put_blocks(first.x, t, q, outer((r["fkh"], r["fkl"]), (r["vh"], r["vl"]), t, q))
        total = jnp.sum(r["fk"][moments[t], :], axis=0, keepdims=True)
        for p in range(PAIRS):
            put_row(first.x, t, p, total[:, 128 * p : 128 * p + 128])

    pl.semaphore_wait(barrier, len(everyone))
    first.start_core()
    wq_ref = fetched("wq")
    r["uq"][...] = dot(rows, wq_ref[...]) * FACTOR
    first.start_y()
    for q in range(2):
        fq = features(r["uq"], q)
        r["fq"][:, quads[q]] = fq
        r["fqh"][:, quads[q]], r["fql"][:, quads[q]] = split(fq)
    first.start_z()
    masked = jnp.where(valid, fetched("cot")[...].reshape(ROWS, D), jnp.zeros((), BF16))
    r["gh"][...] = dot_nt(masked, fetched("down")[...])
    up_ref = fetched("up")
    for n in ("sh", "sl", "gsh", "gsl"):
        r[n][...] = jnp.zeros_like(r[n])
    first.start_z_back()
    line = lax.broadcasted_iota(jnp.int32, (QUAD, D), 0)
    column = lax.broadcasted_iota(jnp.int32, (QUAD, D), 1)
    for k in range(2):
        source = (line // 64) * 128 + lax.rem(line // 4, ZS) * 8 + 4 * k + lax.rem(line, 4)
        pick = jnp.where(source == column, 1.0, 0.0).astype(BF16)
        r["turn"][k] = dot_nt(pick, rows).astype(BF16)
    first.start_y_back()
    first.start_core_back()
    first.finish()

    for t in range(T):
        for q in range(2):
            here = moments[t], quads[q]
            get_blocks(first.out, t, q, r["sh"], r["sl"])
            numer = dot3(dot, (r["fqh"][here], r["fql"][here]), (r["sh"][t, q], r["sl"][t, q]))
            inverse = 1.0 / head_sum(r["fq"][here] * get_row(first.out, t, q), ones[...])
            r["rden"][here] = inverse
            r["att"][here] = numer * inverse
    att = r["att"][...]
    rms_inverse = 1.0 / jnp.sqrt(jnp.mean(att * att, axis=1, keepdims=True) + 1e-06)
    normed = att * rms_inverse
    pre = dot(normed.astype(BF16), up_ref[...])
    grad_pre = (r["gh"][...] * gelu_slope(pre)).astype(BF16)
    grad_normed = dot_nt(grad_pre, up_ref[...])
    mean = jnp.mean(grad_normed * normed, axis=1, keepdims=True)
    grad_att = (grad_normed - normed * mean) * rms_inverse
    for q in range(2):
        ga = grad_att[:, QUAD * q : QUAD * q + QUAD]
        inverse = r["rden"][:, quads[q]]
        gnum = ga * inverse
        r["gnum"][:, quads[q]] = gnum
        r["gnh"][:, quads[q]], r["gnl"][:, quads[q]] = split(gnum)
        r["gden"][:, quads[q]] = -head_sum(ga * r["att"][:, quads[q]], ones[...]) * inverse
    for t in range(T):
        for q in range(2):
            put_blocks(second.x, t, q, outer((r["fqh"], r["fql"]), (r["gnh"], r["gnl"]), t, q))
        total = jnp.sum(r["fq"][moments[t], :] * r["gden"][moments[t], :], axis=0, keepdims=True)
        for p in range(PAIRS):
            put_row(second.x, t, p, total[:, 128 * p : 128 * p + 128])

    second.start_core()
    for t in range(T):
        for q in range(2):
            here = moments[t], quads[q]
            gfq = dot3(dot_nt, (r["gnh"][here], r["gnl"][here]), (r["sh"][t, q], r["sl"][t, q]))
            gfq = gfq + r["gden"][here] * get_row(first.out, t, q)
            r["wtd"][here] = gfq * r["fq"][here]
    second.start_y()
    for q in range(2):
        r["gq"][:, quads[q]] = feature_back(r["wtd"][:, quads[q]], r["uq"][:, quads[q]], q)
    job_q, job_k, job_v = (Scatter(pos, peers, r, tag) for tag in ("_q", "_k", "_v"))
    job_q.put("send", dot(r["turn"][1 - c], r["gq"][...]))
    second.start_z()
    job_q.start_core()
    job_q.put("own", dot(r["turn"][c], r["gq"][...]))
    job_q.start_second()
    r["gin"][...] = dot_nt(r["gq"][...], wq_ref[...])
    second.start_z_back()
    second.start_y_back()
    job_q.start_third()
    second.start_core_back()
    second.finish()

    for t in range(T):
        for q in range(2):
            here = moments[t], quads[q]
            get_blocks(second.out, t, q, r["gsh"], r["gsl"])
            blocks = (r["gsh"][t, q], r["gsl"][t, q])
            r["gv"][here] = dot3(dot, (r["fkh"][here], r["fkl"][here]), blocks).astype(BF16)
    job_v.put("send", dot(r["turn"][1 - c], r["gv"][...]))
    job_v.start_core()
    for t in range(T):
        for q in range(2):
            here = moments[t], quads[q]
            blocks = (r["gsh"][t, q], r["gsl"][t, q])
            gfk = dot3(dot_nt, (r["vh"][here], r["vl"][here]), blocks) + get_row(second.out, t, q)
            r["wtd"][here] = gfk * r["fk"][here]
    for q in range(2):
        r["gk"][:, quads[q]] = feature_back(r["wtd"][:, quads[q]], r["uk"][:, quads[q]], q)
    job_k.put("send", dot(r["turn"][1 - c], r["gk"][...]))
    job_k.start_core()
    job_q.start_last()
    job_v.put("own", dot(r["turn"][c], r["gv"][...]))
    job_v.start_second()
    job_k.put("own", dot(r["turn"][c], r["gk"][...]))
    job_k.start_second()
    total = r["gin"][...] + dot_nt(r["gk"][...], r["in_wk"][...]) + dot_nt(r["gv"][...], r["in_wv"][...])
    r["gout"][...] = total.astype(BF16).reshape(T, N, D)
    leave = pltpu.make_async_copy(r["gout"], gin_ref, r["fetch"].at[len(STAGED)])
    leave.start()
    job_v.start_third()
    job_k.start_third()
    job_v.start_last()
    job_k.start_last()
    job_q.finish(oq_ref, scale)
    job_v.finish(ov_ref, scale)
    job_k.finish(ok_ref, scale)
    for job in (first, second, job_q, job_k, job_v):
        job.drain()
    leave.wait()


def hand_on(*refs):
    for source, target in zip(refs[:4], refs[4:]):
        target[...] = source[...]


def shards(inputs, cotangent, w_query, w_key, w_value, w_up, w_down, feature_proj, live_count):
    total_rows = T * XS * N * YS * ZS * 2
    piece = jax.ShapeDtypeStruct((4, 128), F32)
    shapes = (jax.ShapeDtypeStruct((T, N, D), BF16), piece, piece, piece)
    results = pl.pallas_call(
        functools.partial(kernel, 1.0 / math.sqrt(total_rows)),
        out_shape=shapes,
        in_specs=[ANY] * 8 + [SM],
        out_specs=(ANY, VM, VM, VM),
        scratch_shapes=list(scratch().values()),
        compiler_params=pltpu.CompilerParams(collective_id=0, has_side_effects=True, vmem_limit_bytes=56 << 20),
    )(inputs, cotangent, w_query, w_key, w_value, w_up, w_down, feature_proj, live_count)
    return pl.pallas_call(
        hand_on,
        out_shape=shapes,
        in_specs=[VM] * 4,
        out_specs=(VM,) * 4,
    )(*results)


def solution(mesh):
    placed = (P("step", "sensor", None),) * 2 + (P(),) * 6 + (P("sensor"),)
    return jax.shard_map(
        shards,
        mesh=mesh,
        in_specs=placed,
        out_specs=(P("step", "sensor", None),) + (P("sensor", "step"),) * 3,
        check_vma=False,
    )
```
